32 devices in a mesh: span: 2 (over y), tm: 16 (over z, x, core).
Axes of the slice: x: 2, y: 2, z: 4, core: 2. Of those that a mesh axis runs over, the one named last changes fastest.
Arguments:
- traces: bfloat16 [1024, 32768], P(None, ('span', 'tm')), parts along dimension 1, may hold values from -6 to 6
- templates: bfloat16 [256, 16, 512], P('tm'), may hold values from -6 to 6
- blocks: int32 [16, 4], replicated, may hold values from 0 to 7, all different within a row
Outputs:
- detection: float32 [16, 32768], P(None, ('span', 'tm')), parts along dimension 1
The draws below stay inside these ranges and needn't reach their ends.
There are 2 independent parts, one for each index of `span`. The reference program is written for one: setup_inputs(seed, part) draws one part's arguments, and reference() takes and returns one part's arrays. A program takes and returns all parts, laid end to end along the dimension named above; an argument that names none is the same for every part. Nothing has to cross between parts.
Inputs may be any that keep to these rules, and one draw needn't show every extreme that they name: Each row lists 4 different channel blocks.
All inputs are finite; a program needn't handle non-finite values.
Results may differ from the reference program's by a relative error of at most 0.0003.
Values may be sent and summed in bfloat16 or wider, within the bound.
No kernel may reach another device: no remote copies, remote signals or barrier semaphores. Data moves between devices by JAX's collectives and lax.ppermute only.
A program may use at most 128 MiB of HBM per device.

```python
import math
import jax
import jax.numpy as jnp
from jax import lax

C = 1024
MAXB = 4
K = 256
J = 16
NB = 8
R = 512
NT = 16384
N_TM = 16


def steps_of(key, dims, pieces, least, top_value):
    loudness = 1.0
    for axis_at, parts in pieces:
        steps = jax.random.uniform(jax.random.fold_in(jax.random.fold_in(key, 6), axis_at), (parts,), jnp.float32, least / len(pieces), top_value / len(pieces))
        loudness = loudness * jnp.repeat(jnp.exp(steps), dims[axis_at] // parts).reshape((-1,) + (1,) * (len(dims) - 1 - axis_at))
    return loudness


def distinct(own_key, rows, count, top, lift):
    sequence = jax.random.permutation(jax.random.fold_in(own_key, 1), count)
    pull = sequence
    for power in range(3):
        pull = pull * pull // count
    pull = pull * lift // count
    lots = jax.random.randint(jax.random.fold_in(own_key, 2), (rows, count), 0, 4096) + pull
    holders = jax.random.permutation(jax.random.fold_in(own_key, 3), rows)[jnp.arange(count) % rows]
    lots = jnp.where(jnp.arange(rows)[:, None] == holders[None, :], 1 << 14, lots)
    priority = lots * count + jnp.arange(count)
    return lax.top_k(priority.astype(jnp.int32), top)[1].astype(jnp.int32)


def scatter_about(rng, dims, spread, reach, shards=(), kind=jnp.bfloat16):
    array = spread * jax.random.normal(rng, dims, jnp.float32)
    if shards:
        array = array * steps_of(rng, dims, shards, -0.22, 0.18)
    return jnp.clip(array, -reach, reach).astype(kind)


def setup_inputs(seed: int = 0, part: int = 0) -> dict:
    streams_of = jax.random.split(jax.random.key(seed), 4)
    part_splits = jax.random.split(jax.random.fold_in(streams_of[3], part), 4)
    return {
        "traces": scatter_about(part_splits[0], (C, NT), 1.0, 6.0, ((1, 16),)),
        "templates": scatter_about(streams_of[1], (K, J, R), 1.0, 6.0, ((0, 16),)),
        "blocks": distinct(streams_of[2], J, NB, MAXB, 0),
    }


epsilon = 1e-06

def sheared_sum(product, lag_count):
    members, tap_count, span_width = product.shape
    flattened = product.reshape(members, tap_count * span_width)
    flattened = jnp.pad(flattened, ((0, 0), (0, tap_count)))
    return flattened.reshape(members, tap_count, span_width + 1)[:, :, :lag_count].sum(axis=1)

def reference(traces, templates, blocks):
    channels, total = traces.shape
    tap_count, members, row_count = templates.shape
    listed = blocks.shape[1]
    block_rows = row_count // listed
    nblocks = channels // block_rows
    lag_count = total // N_TM
    span_width = lag_count + tap_count
    padded = jnp.pad(traces, ((0, 0), (0, tap_count)))
    starts = jnp.arange(N_TM, dtype=jnp.int32) * lag_count
    selector = (blocks[:, :, None] == jnp.arange(nblocks, dtype=jnp.int32)[None, None, :]).astype(jnp.float32)
    counting = selector.sum(axis=1)
    weights_wide = templates.astype(jnp.float32)
    norm_sums = lax.optimization_barrier(jnp.sum(jnp.square(weights_wide), axis=(0, 2)))
    scale_factor = math.sqrt(tap_count * row_count)

    def one_block(start):
        extended = lax.dynamic_slice(padded, (jnp.int32(0), start), (channels, span_width))
        squares = jnp.square(extended.astype(jnp.float32)).reshape(nblocks, block_rows, span_width).sum(axis=1)
        running = jnp.concatenate([jnp.zeros((nblocks, 1), jnp.float32), jnp.cumsum(squares, axis=1)], axis=1)
        window = running[:, tap_count:tap_count + lag_count] - running[:, :lag_count]
        energy = jnp.dot(counting, window, precision=lax.Precision.HIGHEST)
        chosen = extended.reshape(nblocks, block_rows, span_width)[blocks]
        chosen = chosen.reshape(members, row_count, span_width).astype(jnp.float32)
        product = jnp.einsum('kqr,qrl->qkl', weights_wide, chosen, precision=lax.Precision.HIGHEST)
        correlation = sheared_sum(product, lag_count)
        denominator = energy * norm_sums[:, None] + epsilon
        return correlation * lax.rsqrt(denominator) * scale_factor
    stacked = lax.map(one_block, starts)
    return jnp.transpose(stacked, (1, 0, 2)).reshape(members, total)
```

```python
import math

import jax
import jax.numpy as jnp
from jax import lax
from jax.experimental import pallas as pl
from jax.experimental.pallas import tpu as pltpu
from jax.sharding import PartitionSpec as P

template_groups = 4
epsilon = 1e-06
LANES = 128
SUB = 8


def from_behind(block, axis, distance):
    devices = range(lax.axis_size(axis))
    route = [(i - distance, i) for i in devices if i - distance in devices]
    return lax.ppermute(block, axis, route)


def tap_total(product, lag_count):
    members, tap_count, span_width = product.shape
    flattened = product.reshape(members, tap_count * span_width)
    flattened = jnp.pad(flattened, ((0, 0), (0, tap_count)))
    return flattened.reshape(members, tap_count, span_width + 1)[:, :, :lag_count].sum(axis=1)


def per_device_general(traces, templates, blocks):
    channels, lag_count = traces.shape
    local_taps, members, row_count = templates.shape
    listed = blocks.shape[1]
    block_rows = row_count // listed
    nblocks = channels // block_rows
    tap_count = local_taps * lax.axis_size("tm")
    incoming = from_behind(traces[:, :tap_count], "tm", -1)
    source = jnp.concatenate([traces, incoming], axis=1)
    span_width = source.shape[1]
    squares = (
        jnp.square(source.astype(jnp.float32)).reshape(nblocks, block_rows, span_width).sum(axis=1)
    )
    running = jnp.concatenate(
        [jnp.zeros((nblocks, 1), jnp.float32), jnp.cumsum(squares, axis=1)], axis=1
    )
    window = running[:, tap_count : tap_count + lag_count] - running[:, :lag_count]
    selector = (blocks[:, :, None] == jnp.arange(nblocks, dtype=jnp.int32)[None, None, :]).astype(
        jnp.float32
    )
    counting = selector.sum(axis=1)
    scale_factor = math.sqrt(tap_count * row_count)
    group_size = members // template_groups
    gathered = lax.all_gather(templates, "tm", axis=0, tiled=True)
    pieces = []
    norm_pieces = []
    for group_index in range(template_groups):
        offset = group_index * group_size
        weights = gathered[:, offset : offset + group_size]
        chosen = source.reshape(nblocks, block_rows, span_width)[
            blocks[offset : offset + group_size]
        ]
        chosen = chosen.reshape(group_size, row_count, span_width)
        product = jnp.einsum("kqr,qrl->qkl", weights, chosen, preferred_element_type=jnp.float32)
        pieces.append(tap_total(product, lag_count))
        norm_pieces.append(jnp.sum(jnp.square(weights.astype(jnp.float32)), axis=(0, 2)))
    correlation = jnp.concatenate(pieces, axis=0)
    norm_sums = jnp.concatenate(norm_pieces, axis=0)
    energy = jnp.dot(counting, window, precision=lax.Precision.HIGHEST)
    denominator = energy * norm_sums[:, None] + epsilon
    return correlation * lax.rsqrt(denominator) * scale_factor


ANY = pl.BlockSpec(memory_space=pl.ANY)
SMEM = pl.BlockSpec(memory_space=pltpu.SMEM)


def roll_left(value, distance):
    width = value.shape[-1]
    return pltpu.roll(value, (width - distance) % width, axis=1)


def arrange(own, partner):
    taps, members, rows = own.shape
    half = members // 2
    chip_taps = 2 * taps
    flat = taps * members

    def kernel(own_ref, partner_ref, out_ref):
        core = lax.axis_index("tm") % 2
        shape = (half * chip_taps, flat)
        row = lax.broadcasted_iota(jnp.int32, shape, 0)
        source = lax.broadcasted_iota(jnp.int32, shape, 1)
        member = row // chip_taps
        place = row % chip_taps
        tap = place + (SUB - 1) - 2 * (place % SUB)
        wanted = (tap % taps) * members + half * core + member
        hit = source == wanted
        mine = (tap // taps) == core
        pick_own = jnp.where(hit & mine, 1.0, 0.0).astype(jnp.bfloat16)
        pick_partner = jnp.where(hit & jnp.logical_not(mine), 1.0, 0.0).astype(jnp.bfloat16)
        picked = jnp.dot(pick_own, own_ref[...], preferred_element_type=jnp.float32)
        picked += jnp.dot(pick_partner, partner_ref[...], preferred_element_type=jnp.float32)
        out_ref[...] = picked.astype(jnp.bfloat16)

    out = pl.pallas_call(
        kernel,
        out_shape=jax.ShapeDtypeStruct((half * chip_taps, rows), jnp.bfloat16),
        name="arrange",
    )(own.reshape(flat, rows), partner.reshape(flat, rows))
    return out.reshape(half, chip_taps, rows)


def window_sums(own, partner, nblocks, tap_count):
    channels, lags = own.shape
    rows = channels // nblocks
    width = tap_count + 2 * lags

    def kernel(own_ref, partner_ref, out_ref, sums):
        core = lax.axis_index("tm") % 2
        sums[:, :tap_count] = jnp.zeros((nblocks, tap_count), jnp.float32)
        for b in range(nblocks):
            mine = jnp.sum(jnp.square(own_ref[b * rows : (b + 1) * rows, :].astype(jnp.float32)), axis=0, keepdims=True)
            other = jnp.sum(jnp.square(partner_ref[b * rows : (b + 1) * rows, :].astype(jnp.float32)), axis=0, keepdims=True)
            sums[b : b + 1, tap_count : tap_count + lags] = jnp.where(core == 0, mine, other)
            sums[b : b + 1, tap_count + lags :] = jnp.where(core == 0, other, mine)
        total = sums[...]
        distance = 1
        while distance < tap_count:
            total = total + roll_left(total, distance)
            distance *= 2
        out_ref[...] = total

    return pl.pallas_call(
        kernel,
        out_shape=jax.ShapeDtypeStruct((nblocks, width), jnp.float32),
        scratch_shapes=[pltpu.VMEM((nblocks, width), jnp.float32)],
        name="window_sums",
    )(own, partner)


def correlate_body(blocks_ref, x_own, x_partner, units, xs, ws, ps, sem_x, sem_w, norm_out, emit):
    core = lax.axis_index("tm") % 2
    groups, half, chip_taps, rows = ws.shape
    taps = groups * chip_taps
    _, channels, lags = xs.shape
    listed = blocks_ref.shape[1]
    block_rows = rows // listed
    copies = [
        pltpu.make_async_copy(ref, ws.at[place, pl.ds(first, count)], sem_w.at[n])
        for n, (ref, place, first, count) in enumerate(units)
    ]
    copies += [
        pltpu.make_async_copy(x_own, xs.at[core], sem_x.at[0]),
        pltpu.make_async_copy(x_partner, xs.at[1 - core], sem_x.at[1]),
    ]
    for copy in copies:
        copy.start()
    pad = jnp.zeros((taps, taps), jnp.float32)
    for p in ps:
        p[:, :taps] = pad
        p[:, taps + 2 * lags :] = pad
    for copy in copies:
        copy.wait()

    def multiply(j, p):
        weights = ws[:, j].reshape(taps, rows)
        for r in range(2):
            chosen = jnp.concatenate(
                [
                    xs[r, pl.ds(pl.multiple_of(blocks_ref[half * core + j, m] * block_rows, block_rows), block_rows), :]
                    for m in range(listed)
                ],
                axis=0,
            )
            p[:, taps + r * lags : taps + (r + 1) * lags] = jnp.dot(
                weights, chosen, preferred_element_type=jnp.float32
            )
        squares = jnp.square(weights.astype(jnp.float32)).sum(axis=0, keepdims=True)
        folded = squares[:, :LANES]
        for n in range(1, rows // LANES):
            folded = folded + squares[:, n * LANES : (n + 1) * LANES]
        norm_out(j, folded)

    def shear(j, p):
        width = taps + 2 * lags
        step = 4 * LANES
        for low in range(0, width, step):
            size = min(step, width - low)

            def tree(first, count):
                if count == 1:
                    return p[first * SUB : (first + 1) * SUB, low : low + size + taps]
                part = count // 2
                return tree(first, part) + roll_left(tree(first + part, part), part * SUB)

            emit(j, low, tree(0, taps // SUB)[:, :size])

    for j in range(half):
        multiply(j, ps[j % 2])
        if j > 0:
            shear(j - 1, ps[(j - 1) % 2])
    shear(half - 1, ps[(half - 1) % 2])


def near_half(blocks, x_own, x_partner, units):
    half, chip_taps, rows = units[0].shape
    groups = len(units)
    taps = groups * chip_taps
    channels, lags = x_own.shape

    def kernel(blocks_ref, xo, xp, u0, u1, u2, u3, r_ref, n_ref, xs, ws, p0, p1, sem_x, sem_w):
        chip = lax.axis_index("tm") // 2
        place = chip % groups
        listing = [(u0, place, 0, half), (u1, place ^ 1, 0, half), (u2, place ^ 2, 0, half), (u3, place ^ 3, 0, half)]

        def norm_out(j, folded):
            n_ref[j : j + 1, :] = folded

        def emit(j, low, value):
            r_ref[j, :, low : low + value.shape[1]] = value

        correlate_body(blocks_ref, xo, xp, listing, xs, ws, (p0, p1), sem_x, sem_w, norm_out, emit)

    return pl.pallas_call(
        kernel,
        out_shape=(
            jax.ShapeDtypeStruct((half, SUB, taps + 2 * lags), jnp.float32),
            jax.ShapeDtypeStruct((half, LANES), jnp.float32),
        ),
        in_specs=[SMEM] + [ANY] * 6,
        scratch_shapes=[
            pltpu.VMEM((2, channels, lags), jnp.bfloat16),
            pltpu.VMEM((groups, half, chip_taps, rows), jnp.bfloat16),
            pltpu.VMEM((taps, 2 * taps + 2 * lags), jnp.float32),
            pltpu.VMEM((taps, 2 * taps + 2 * lags), jnp.float32),
            pltpu.SemaphoreType.DMA((2,)),
            pltpu.SemaphoreType.DMA((4,)),
        ],
        name="near_half",
    )(blocks, x_own, x_partner, *units)


def far_half(blocks, x_own, x_partner, units, near, near_norm, window):
    half, chip_taps, rows = units[0].shape
    groups = 4
    taps = groups * chip_taps
    channels, lags = x_own.shape
    tap_count = 2 * taps
    width = tap_count + 2 * lags

    def kernel(blocks_ref, xo, xp, u0, u1, u2, u3, u4, near_ref, nn_ref, w_ref,
               keep_ref, norm_ref, send_ref, pre_ref, xs, ws, p0, p1, fs, r_ref, sem_x, sem_w):
        core = lax.axis_index("tm") % 2
        chip = lax.axis_index("tm") // 2
        near_first = (chip // groups) % 2 == 0
        place = (chip % groups) ^ (2 * lax.axis_index("span"))
        listing = [
            (u0, place, 0, half), (u1, place ^ 1, 0, half), (u2, place ^ 2, 0, half),
            (u3, place ^ 3, 0, half // 2), (u4, place ^ 3, half // 2, half // 2),
        ]

        def norm_out(j, folded):
            norm_ref[j : j + 1, :] = folded + nn_ref[j : j + 1, :]

        def finish(j):
            zeros = jnp.zeros((SUB, taps), jnp.float32)
            a = near_ref[j]
            b = r_ref[j % 2]
            first = jnp.where(near_first, a, b)
            second = jnp.where(near_first, b, a)
            rows8 = jnp.concatenate([zeros, first], axis=1) + jnp.concatenate([second, zeros], axis=1)
            sub = lax.broadcasted_iota(jnp.int32, (SUB, width), 0)
            delay = (SUB - 1) - sub
            distance = 1
            while distance < SUB:
                rows8 = jnp.where((delay & distance) != 0, roll_left(rows8, distance), rows8)
                distance *= 2
            fs[j : j + 1, :] = jnp.sum(rows8, axis=0, keepdims=True)

        def emit(j, low, value):
            r_ref[j % 2, :, low : low + value.shape[1]] = value
            if low + value.shape[1] == taps + 2 * lags:
                finish(j)

        correlate_body(blocks_ref, xo, xp, listing, xs, ws, (p0, p1), sem_x, sem_w, norm_out, emit)
        lag0 = fs[:, tap_count : tap_count + lags]
        lag1 = fs[:, tap_count + lags :]
        keep_ref[...] = jnp.where(core == 0, lag0, lag1)
        send_ref[:, :lags] = jnp.where(core == 0, lag1, lag0)
        send_ref[:, lags:] = norm_ref[...]
        pre_ref[:half, :] = fs[:, :tap_count]
        pre_ref[half:, :] = w_ref[:, :tap_count]

    return pl.pallas_call(
        kernel,
        out_shape=(
            jax.ShapeDtypeStruct((half, lags), jnp.float32),
            jax.ShapeDtypeStruct((half, LANES), jnp.float32),
            jax.ShapeDtypeStruct((half, lags + LANES), jnp.float32),
            jax.ShapeDtypeStruct((half + window.shape[0], tap_count), jnp.float32),
        ),
        in_specs=[SMEM] + [ANY] * 7 + [pl.BlockSpec(memory_space=pltpu.VMEM)] * 3,
        scratch_shapes=[
            pltpu.VMEM((2, channels, lags), jnp.bfloat16),
            pltpu.VMEM((groups, half, chip_taps, rows), jnp.bfloat16),
            pltpu.VMEM((taps, 2 * taps + 2 * lags), jnp.float32),
            pltpu.VMEM((taps, 2 * taps + 2 * lags), jnp.float32),
            pltpu.VMEM((half, width), jnp.float32),
            pltpu.VMEM((2, SUB, taps + 2 * lags), jnp.float32),
            pltpu.SemaphoreType.DMA((2,)),
            pltpu.SemaphoreType.DMA((5,)),
        ],
        name="far_half",
    )(blocks, x_own, x_partner, *units, near, near_norm, window)


def finish(blocks, keep, norm, received, window, before_a, before_b, scale_factor):
    half, lags = keep.shape
    members, listed = blocks.shape
    nblocks, width = window.shape
    tap_count = width - 2 * lags

    def kernel(blocks_ref, keep_ref, norm_ref, recv_ref, w_ref, a_ref, b_ref, out_ref, win, energy):
        core = lax.axis_index("tm") % 2
        tail = lags - tap_count
        win[...] = jnp.where(core == 0, w_ref[:, tap_count : tap_count + lags], w_ref[:, tap_count + lags :])
        win[:, tail:] = win[:, tail:] + a_ref[half:, :]
        for j in range(members):
            total = win[pl.ds(blocks_ref[j, 0], 1), :]
            for m in range(1, listed):
                total = total + win[pl.ds(blocks_ref[j, m], 1), :]
            energy[j : j + 1, :] = total

        def place(row, value_ref, tail_ref, norms):
            sums = jnp.sum(norms, axis=1, keepdims=True)
            start = pl.multiple_of(row * half, half)
            factor = lax.rsqrt(energy[pl.ds(start, half), :] * sums + epsilon) * scale_factor
            out_ref[pl.ds(start, half), :tail] = value_ref[:, :tail] * factor[:, :tail]
            out_ref[pl.ds(start, half), tail:] = (
                value_ref[:, tail:lags] + tail_ref[:half, :]
            ) * factor[:, tail:]

        place(core, keep_ref, b_ref, norm_ref[...])
        place(1 - core, recv_ref, a_ref, recv_ref[:, lags:])

    return pl.pallas_call(
        kernel,
        out_shape=jax.ShapeDtypeStruct((members, lags), jnp.float32),
        in_specs=[SMEM] + [pl.BlockSpec(memory_space=pltpu.VMEM)] * 6,
        scratch_shapes=[
            pltpu.VMEM((nblocks, lags), jnp.float32),
            pltpu.VMEM((members, lags), jnp.float32),
        ],
        name="finish",
    )(blocks, keep, norm, received, window, before_a, before_b)


def per_device_chips(traces, templates, blocks):
    channels, lag_count = traces.shape
    local_taps, members, row_count = templates.shape
    block_rows = row_count // blocks.shape[1]
    nblocks = channels // block_rows
    spans = lax.axis_size("span")
    count = lax.axis_size("tm")
    tap_count = local_taps * count
    both = ("span", "tm")

    def send(value, target):
        route = []
        for s in range(spans):
            for i in range(count):
                to = target(s, i)
                if to is not None:
                    route.append((s * count + i, to[0] * count + to[1]))
        return lax.ppermute(value, both, route)

    def over_core(value):
        return send(value, lambda s, i: (s, i ^ 1))

    def over_x(value):
        return send(value, lambda s, i: (s, i ^ 2))

    def over_y(value):
        return send(value, lambda s, i: (s ^ 1, i))

    own = arrange(templates, over_core(templates))
    x_partner = over_core(traces)
    half = members // 2
    own_x = over_x(own)
    far = send(own, lambda s, i: (s, i ^ (8 if s == 0 else 12)))
    near = send(own, lambda s, i: (s, i ^ 4))
    near_x = over_x(near)
    far_x = over_x(far)
    far_y = over_y(far)
    far_xy_0 = over_x(far_y[: half // 2])
    far_xy_1 = over_y(far_x[half // 2 :])

    window = window_sums(traces, x_partner, nblocks, tap_count)
    sheared, near_norm = near_half(blocks, traces, x_partner, (own, own_x, near, near_x))
    keep, norm, outgoing, before = far_half(
        blocks, traces, x_partner, (far, far_x, far_y, far_xy_0, far_xy_1), sheared, near_norm, window
    )

    def back(core):
        return lambda s, i: (s, i - 2 + (1 - core)) if i >= 2 and i % 2 == core else None

    before_a = send(before, back(0))
    before_b = send(before, back(1))
    received = over_core(outgoing)
    return finish(
        blocks, keep, norm, received, window, before_a, before_b, math.sqrt(tap_count * row_count)
    )


def fits(mesh, traces, templates, blocks):
    spans, count = mesh.shape["span"], mesh.shape["tm"]
    taps, members, rows = templates.shape
    local_taps = taps // count
    lags = traces.shape[1] // (spans * count)
    block_rows = rows // blocks.shape[1]
    return (
        spans == 2
        and count == 16
        and members == 16
        and local_taps == 16
        and lags % 512 == 0
        and lags >= taps
        and block_rows % 128 == 0
        and traces.shape[0] // block_rows == 8
    )


def solution(mesh):
    def program(traces, templates, blocks):
        body = per_device_chips if fits(mesh, traces, templates, blocks) else per_device_general
        return jax.shard_map(
            body,
            mesh=mesh,
            in_specs=(P(None, ("span", "tm")), P("tm", None, None), P()),
            out_specs=P(None, ("span", "tm")),
            check_vma=False,
        )(traces, templates, blocks)

    return program
```

```python
import math

import jax
import jax.numpy as jnp
from jax import lax
from jax.experimental import pallas as pl
from jax.experimental.pallas import tpu as pltpu
from jax.sharding import PartitionSpec as P

template_groups = 4
epsilon = 1e-06
LANES = 128
SUB = 8


def from_behind(block, axis, distance):
    devices = range(lax.axis_size(axis))
    route = [(i - distance, i) for i in devices if i - distance in devices]
    return lax.ppermute(block, axis, route)


def tap_total(product, lag_count):
    members, tap_count, span_width = product.shape
    flattened = product.reshape(members, tap_count * span_width)
    flattened = jnp.pad(flattened, ((0, 0), (0, tap_count)))
    return flattened.reshape(members, tap_count, span_width + 1)[:, :, :lag_count].sum(axis=1)


def per_device_general(traces, templates, blocks):
    channels, lag_count = traces.shape
    local_taps, members, row_count = templates.shape
    listed = blocks.shape[1]
    block_rows = row_count // listed
    nblocks = channels // block_rows
    tap_count = local_taps * lax.axis_size("tm")
    incoming = from_behind(traces[:, :tap_count], "tm", -1)
    source = jnp.concatenate([traces, incoming], axis=1)
    span_width = source.shape[1]
    squares = (
        jnp.square(source.astype(jnp.float32)).reshape(nblocks, block_rows, span_width).sum(axis=1)
    )
    running = jnp.concatenate(
        [jnp.zeros((nblocks, 1), jnp.float32), jnp.cumsum(squares, axis=1)], axis=1
    )
    window = running[:, tap_count : tap_count + lag_count] - running[:, :lag_count]
    selector = (blocks[:, :, None] == jnp.arange(nblocks, dtype=jnp.int32)[None, None, :]).astype(
        jnp.float32
    )
    counting = selector.sum(axis=1)
    scale_factor = math.sqrt(tap_count * row_count)
    group_size = members // template_groups
    gathered = lax.all_gather(templates, "tm", axis=0, tiled=True)
    pieces = []
    norm_pieces = []
    for group_index in range(template_groups):
        offset = group_index * group_size
        weights = gathered[:, offset : offset + group_size]
        chosen = source.reshape(nblocks, block_rows, span_width)[
            blocks[offset : offset + group_size]
        ]
        chosen = chosen.reshape(group_size, row_count, span_width)
        product = jnp.einsum("kqr,qrl->qkl", weights, chosen, preferred_element_type=jnp.float32)
        pieces.append(tap_total(product, lag_count))
        norm_pieces.append(jnp.sum(jnp.square(weights.astype(jnp.float32)), axis=(0, 2)))
    correlation = jnp.concatenate(pieces, axis=0)
    norm_sums = jnp.concatenate(norm_pieces, axis=0)
    energy = jnp.dot(counting, window, precision=lax.Precision.HIGHEST)
    denominator = energy * norm_sums[:, None] + epsilon
    return correlation * lax.rsqrt(denominator) * scale_factor


ANY = pl.BlockSpec(memory_space=pl.ANY)
SMEM = pl.BlockSpec(memory_space=pltpu.SMEM)
VMEM = pl.BlockSpec(memory_space=pltpu.VMEM)
PARAMS = pltpu.CompilerParams(vmem_limit_bytes=24 << 20)


def resident(value):
    return pltpu.with_memory_space_constraint(value, pltpu.VMEM)


def roll_left(value, distance):
    width = value.shape[-1]
    return pltpu.roll(value, (width - distance) % width, axis=1)


def energies(listing, traces, members, nblocks, tap_count):
    channels, lags = traces.shape
    rows = channels // nblocks
    listed = listing.shape[0]
    width = tap_count + lags

    def kernel(listing_ref, x_ref, before_ref, own_ref, sums):
        sums[:, :tap_count] = jnp.zeros((nblocks, tap_count), jnp.float32)
        for b in range(nblocks):
            block = x_ref[b * rows : (b + 1) * rows, :].astype(jnp.float32)
            sums[b : b + 1, tap_count:] = jnp.sum(jnp.square(block), axis=0, keepdims=True)
        total = sums[...]
        distance = 1
        while distance < tap_count:
            total = total + roll_left(total, distance)
            distance *= 2
        sums[...] = total
        for j in range(members):
            energy = sums[pl.ds(listing_ref[0, j], 1), :]
            for m in range(1, listed):
                energy = energy + sums[pl.ds(listing_ref[m, j], 1), :]
            before_ref[j : j + 1, :] = energy[:, :tap_count]
            own_ref[j : j + 1, :] = energy[:, tap_count:]

    return pl.pallas_call(
        kernel,
        out_shape=(
            pltpu.VMEM((members, tap_count), jnp.float32),
            pltpu.VMEM((members, lags), jnp.float32),
        ),
        in_specs=[SMEM, VMEM],
        out_specs=(VMEM, VMEM),
        scratch_shapes=[pltpu.VMEM((nblocks, width), jnp.float32)],
        compiler_params=PARAMS,
        name="energies",
    )(listing, resident(traces))


def regroup(raw, taps, members):
    count = taps * members
    row = lax.broadcasted_iota(jnp.int32, (count, 1), 0)
    member, tap = row // taps, (row % taps) ^ (SUB - 1)
    wanted = tap * members + member
    source = lax.broadcasted_iota(jnp.int32, (count, count), 1)
    pick = jnp.where(source == wanted, 1.0, 0.0).astype(jnp.bfloat16)
    return [jnp.dot(pick, value, preferred_element_type=jnp.float32).astype(jnp.bfloat16) for value in raw]


def multiply_shear(listing_ref, x_ref, ws, ps, norm_out, emit):
    groups, flat, rows = ws.shape
    listed, members = listing_ref.shape
    local_taps = flat // members
    taps = groups * local_taps
    block_rows = rows // listed
    for p in ps:
        p[:, :taps] = jnp.zeros((taps, taps), jnp.float32)

    def multiply(j, p):
        weights = ws[:, j * local_taps : (j + 1) * local_taps, :].reshape(taps, rows)
        chosen = jnp.concatenate(
            [
                x_ref[pl.ds(pl.multiple_of(listing_ref[m, j] * block_rows, block_rows), block_rows), :]
                for m in range(listed)
            ],
            axis=0,
        )
        p[:, taps:] = jnp.dot(weights, chosen, preferred_element_type=jnp.float32)
        squares = jnp.square(weights.astype(jnp.float32)).sum(axis=0, keepdims=True)
        folded = squares[:, :LANES]
        for n in range(1, rows // LANES):
            folded = folded + squares[:, n * LANES : (n + 1) * LANES]
        norm_out(j, folded)

    def shear(j, p):
        def tree(first, count):
            if count == 1:
                return p[first * SUB : (first + 1) * SUB, :]
            part = count // 2
            return tree(first, part) + roll_left(tree(first + part, part), part * SUB)

        emit(j, tree(0, taps // SUB))

    for j in range(members):
        multiply(j, ps[j % 2])
        if j > 0:
            shear(j - 1, ps[(j - 1) % 2])
    shear(members - 1, ps[(members - 1) % 2])


def scratch(groups, flat, rows, taps, lags):
    return [
        pltpu.VMEM((groups, flat, rows), jnp.bfloat16),
        pltpu.VMEM((taps, taps + lags), jnp.float32),
        pltpu.VMEM((taps, taps + lags), jnp.float32),
    ]


def near_half(listing, traces, units, local_taps, members):
    flat, rows = units[0].shape
    groups = len(units)
    taps = groups * local_taps
    lags = traces.shape[1]

    def kernel(listing_ref, x_ref, *refs):
        inputs, (sheared_ref, norm_ref, ws, p0, p1) = refs[:groups], refs[groups:]
        place = lax.axis_index("tm") % groups
        for n, value in enumerate(regroup([ref[...] for ref in inputs], local_taps, members)):
            ws[place ^ n] = value

        def norm_out(j, folded):
            norm_ref[j : j + 1, :] = folded

        def emit(j, value):
            sheared_ref[j] = value

        multiply_shear(listing_ref, x_ref, ws, (p0, p1), norm_out, emit)

    return pl.pallas_call(
        kernel,
        out_shape=(
            pltpu.VMEM((members, SUB, taps + lags), jnp.float32),
            pltpu.VMEM((members, LANES), jnp.float32),
        ),
        in_specs=[SMEM] + [VMEM] * (1 + groups),
        out_specs=(VMEM, VMEM),
        scratch_shapes=scratch(groups, flat, rows, taps, lags),
        compiler_params=PARAMS,
        name="near_half",
    )(listing, resident(traces), *[resident(unit) for unit in units])


def far_half(listing, traces, units, quarter, near, near_norm, before, local_taps, members):
    flat, rows = units[0].shape
    groups = len(units) + 2
    taps = groups * local_taps
    lags = traces.shape[1]
    tap_count = 2 * taps
    width = tap_count + lags

    def kernel(listing_ref, x_ref, near_ref, nn_ref, before_ref, *refs):
        inputs = refs[: groups + 2]
        main_ref, norm_ref, pre_ref, ws, p0, p1 = refs[groups + 2 :]
        index = lax.axis_index("tm")
        near_first = (index // groups) % 2 == 0
        place = (index % groups) ^ ((groups // 2) * lax.axis_index("span"))
        values = [ref[...] for ref in inputs[: groups - 2]]
        for n in range(2):
            values.append(jnp.concatenate([inputs[groups - 2 + 2 * n][...], inputs[groups - 1 + 2 * n][...]], axis=0))
        for n, value in enumerate(regroup(values, local_taps, members)):
            ws[place ^ n] = value

        def norm_out(j, folded):
            norm_ref[j : j + 1, :] = folded + nn_ref[j : j + 1, :]

        def emit(j, value):
            zeros = jnp.zeros((SUB, taps), jnp.float32)
            a = near_ref[j]
            first = jnp.where(near_first, a, value)
            second = jnp.where(near_first, value, a)
            total = jnp.concatenate([zeros, first], axis=1) + jnp.concatenate([second, zeros], axis=1)
            delay = (SUB - 1) - lax.broadcasted_iota(jnp.int32, (SUB, width), 0)
            distance = 1
            while distance < SUB:
                total = jnp.where((delay & distance) != 0, roll_left(total, distance), total)
                distance *= 2
            line = jnp.sum(total, axis=0, keepdims=True)
            pre_ref[j : j + 1, :] = line[:, :tap_count]
            main_ref[j : j + 1, :] = line[:, tap_count:]

        pre_ref[members:, :] = before_ref[...]
        multiply_shear(listing_ref, x_ref, ws, (p0, p1), norm_out, emit)

    return pl.pallas_call(
        kernel,
        out_shape=(
            pltpu.VMEM((members, lags), jnp.float32),
            pltpu.VMEM((members, LANES), jnp.float32),
            pltpu.VMEM((2 * members, tap_count), jnp.float32),
        ),
        in_specs=[SMEM] + [VMEM] * (4 + groups + 2),
        out_specs=(VMEM,) * 3,
        scratch_shapes=scratch(groups, flat, rows, taps, lags),
        compiler_params=PARAMS,
        name="far_half",
    )(
        listing, resident(traces), resident(near), resident(near_norm), resident(before),
        *[resident(unit) for unit in units], *[resident(part) for part in quarter],
    )


def finish(main, norm, energy, after, scale_factor):
    members, lags = main.shape
    tap_count = after.shape[1]
    tail = lags - tap_count

    def kernel(main_ref, norm_ref, energy_ref, after_ref, out_ref):
        norms = jnp.sum(norm_ref[...], axis=1, keepdims=True)
        factor = lax.rsqrt(energy_ref[:, :tail] * norms + epsilon) * scale_factor
        out_ref[:, :tail] = main_ref[:, :tail] * factor
        factor = lax.rsqrt((energy_ref[:, tail:] + after_ref[members:, :]) * norms + epsilon) * scale_factor
        out_ref[:, tail:] = (main_ref[:, tail:] + after_ref[:members, :]) * factor

    return pl.pallas_call(
        kernel,
        out_shape=jax.ShapeDtypeStruct((members, lags), jnp.float32),
        in_specs=[VMEM] * 4,
        compiler_params=PARAMS,
        name="finish",
    )(resident(main), resident(norm), resident(energy), resident(after))


def per_device_chips(traces, templates, blocks):
    channels, lag_count = traces.shape
    local_taps, members, row_count = templates.shape
    block_rows = row_count // blocks.shape[1]
    nblocks = channels // block_rows
    spans = lax.axis_size("span")
    count = lax.axis_size("tm")
    tap_count = local_taps * count
    both = ("span", "tm")
    listing = blocks.T

    def send(value, target):
        route = []
        for s in range(spans):
            for i in range(count):
                to = target(s, i)
                if to is not None:
                    route.append((s * count + i, to[0] * count + to[1]))
        return lax.ppermute(value, both, route)

    def over_core(value):
        return send(value, lambda s, i: (s, i ^ 1))

    def over_x(value):
        return send(value, lambda s, i: (s, i ^ 2))

    def over_y(value):
        return send(value, lambda s, i: (s ^ 1, i))

    own = templates.reshape(local_taps * members, row_count)
    far = send(own, lambda s, i: (s, i ^ (8 if s == 0 else 12)))
    own_x = over_x(own)
    near = send(own, lambda s, i: (s, i ^ 4))
    near_x = over_x(near)
    far_x = over_x(far)
    far_y = over_y(far)
    part = own.shape[0] // 2
    far_xy_0 = over_x(far_y[:part])
    far_xy_1 = over_y(far_x[part:])

    before, energy = energies(listing, traces, members, nblocks, tap_count)
    units = []
    for unit in (own, own_x, near, near_x):
        units += [unit, over_core(unit)]
    sheared, near_norm = near_half(listing, traces, units, local_taps, members)
    units = []
    for unit in (far, far_x, far_y):
        units += [unit, over_core(unit)]
    quarter = [far_xy_0, far_xy_1, over_core(far_xy_0), over_core(far_xy_1)]
    main, norm, pre = far_half(
        listing, traces, units, quarter, sheared, near_norm, before, local_taps, members
    )
    after = send(pre, lambda s, i: (s, i - 1) if i > 0 else None)
    return finish(main, norm, energy, after, math.sqrt(tap_count * row_count))


def fits(mesh, traces, templates, blocks):
    spans, count = mesh.shape["span"], mesh.shape["tm"]
    taps, members, rows = templates.shape
    local_taps = taps // count
    lags = traces.shape[1] // (spans * count)
    block_rows = rows // blocks.shape[1]
    return (
        spans == 2
        and count == 16
        and members == 16
        and local_taps == 16
        and lags % 512 == 0
        and lags >= taps
        and block_rows % 128 == 0
        and traces.shape[0] // block_rows == 8
    )


def solution(mesh):
    def program(traces, templates, blocks):
        body = per_device_chips if fits(mesh, traces, templates, blocks) else per_device_general
        return jax.shard_map(
            body,
            mesh=mesh,
            in_specs=(P(None, ("span", "tm")), P("tm", None, None), P()),
            out_specs=P(None, ("span", "tm")),
            check_vma=False,
        )(traces, templates, blocks)

    return program
```

```python
import math

import jax
import jax.numpy as jnp
from jax import lax
from jax.experimental import pallas as pl
from jax.experimental.pallas import tpu as pltpu
from jax.sharding import PartitionSpec as P


template_groups = 4
epsilon = 1e-06
LANES = 128


def from_behind(block, axis, distance):
    devices = range(lax.axis_size(axis))
    route = [(i - distance, i) for i in devices if i - distance in devices]
    return lax.ppermute(block, axis, route)


def tap_total(product, lag_count):
    members, tap_count, span_width = product.shape
    flattened = product.reshape(members, tap_count * span_width)
    flattened = jnp.pad(flattened, ((0, 0), (0, tap_count)))
    return flattened.reshape(members, tap_count, span_width + 1)[:, :, :lag_count].sum(axis=1)


def per_device_general(traces, templates, blocks):
    channels, lag_count = traces.shape
    local_taps, members, row_count = templates.shape
    listed = blocks.shape[1]
    block_rows = row_count // listed
    nblocks = channels // block_rows
    tap_count = local_taps * lax.axis_size("tm")
    incoming = from_behind(traces[:, :tap_count], "tm", -1)
    source = jnp.concatenate([traces, incoming], axis=1)
    span_width = source.shape[1]
    squares = (
        jnp.square(source.astype(jnp.float32)).reshape(nblocks, block_rows, span_width).sum(axis=1)
    )
    running = jnp.concatenate(
        [jnp.zeros((nblocks, 1), jnp.float32), jnp.cumsum(squares, axis=1)], axis=1
    )
    window = running[:, tap_count : tap_count + lag_count] - running[:, :lag_count]
    selector = (blocks[:, :, None] == jnp.arange(nblocks, dtype=jnp.int32)[None, None, :]).astype(
        jnp.float32
    )
    counting = selector.sum(axis=1)
    scale_factor = math.sqrt(tap_count * row_count)
    group_size = members // template_groups
    gathered = lax.all_gather(templates, "tm", axis=0, tiled=True)
    pieces = []
    norm_pieces = []
    for group_index in range(template_groups):
        offset = group_index * group_size
        weights = gathered[:, offset : offset + group_size]
        chosen = source.reshape(nblocks, block_rows, span_width)[
            blocks[offset : offset + group_size]
        ]
        chosen = chosen.reshape(group_size, row_count, span_width)
        product = jnp.einsum("kqr,qrl->qkl", weights, chosen, preferred_element_type=jnp.float32)
        pieces.append(tap_total(product, lag_count))
        norm_pieces.append(jnp.sum(jnp.square(weights.astype(jnp.float32)), axis=(0, 2)))
    correlation = jnp.concatenate(pieces, axis=0)
    norm_sums = jnp.concatenate(norm_pieces, axis=0)
    energy = jnp.dot(counting, window, precision=lax.Precision.HIGHEST)
    denominator = energy * norm_sums[:, None] + epsilon
    return correlation * lax.rsqrt(denominator) * scale_factor


SMEM = pl.BlockSpec(memory_space=pltpu.SMEM)
VMEM = pl.BlockSpec(memory_space=pltpu.VMEM)
HBM = pl.BlockSpec(memory_space=pltpu.HBM)
PARAMS = pltpu.CompilerParams(vmem_limit_bytes=24 << 20)


def resident(value):
    return pltpu.with_memory_space_constraint(value, pltpu.VMEM)


def in_hbm(value):
    return pltpu.with_memory_space_constraint(value, pltpu.HBM)


def roll_left(value, distance):
    width = value.shape[-1]
    return pltpu.roll(value, (width - distance) % width, axis=1)


def prepare(listing, traces, own, members, nblocks, tap_count):
    channels, lags = traces.shape
    rows = channels // nblocks
    listed = listing.shape[0]
    width = tap_count + lags

    def kernel(listing_ref, x_hbm, own_hbm, before_ref, energy_ref, mask_ref, x_ref, own_ref, sums, sems):
        copies = [
            pltpu.make_async_copy(x_hbm.at[pl.ds(b * rows, rows)], x_ref.at[pl.ds(b * rows, rows)], sems.at[b])
            for b in range(nblocks)
        ]
        copies.append(pltpu.make_async_copy(own_hbm, own_ref, sems.at[nblocks]))
        for copy in copies:
            copy.start()
        member = lax.broadcasted_iota(jnp.int32, (members, rows), 0)
        for m in range(listed):
            block = jnp.zeros((members, rows), jnp.int32)
            for j in range(members):
                block = jnp.where(member == j, listing_ref[m, j], block)
            for n in range(nblocks):
                mask_ref[m, n] = jnp.where(block == n, 1.0, 0.0).astype(jnp.bfloat16)
        sums[:, :tap_count] = jnp.zeros((nblocks, tap_count), jnp.float32)
        for b in range(nblocks):
            copies[b].wait()
            block = x_ref[b * rows : (b + 1) * rows, :].astype(jnp.float32)
            sums[b : b + 1, tap_count:] = jnp.sum(jnp.square(block), axis=0, keepdims=True)
        total = sums[...]
        distance = 1
        while distance < tap_count:
            total = total + roll_left(total, distance)
            distance *= 2
        sums[...] = total
        for j in range(members):
            energy = sums[pl.ds(listing_ref[0, j], 1), :]
            for m in range(1, listed):
                energy = energy + sums[pl.ds(listing_ref[m, j], 1), :]
            before_ref[j : j + 1, :] = energy[:, :tap_count]
            energy_ref[j : j + 1, :] = energy[:, tap_count:]
        copies[nblocks].wait()

    return pl.pallas_call(
        kernel,
        out_shape=(
            pltpu.VMEM((members, tap_count), jnp.float32),
            pltpu.VMEM((members, lags), jnp.float32),
            pltpu.VMEM((listed, nblocks, members, rows), jnp.bfloat16),
            pltpu.VMEM(traces.shape, traces.dtype),
            pltpu.VMEM(own.shape, own.dtype),
        ),
        in_specs=[SMEM, HBM, HBM],
        out_specs=(VMEM,) * 5,
        scratch_shapes=[pltpu.VMEM((nblocks, width), jnp.float32), pltpu.SemaphoreType.DMA((nblocks + 1,))],
        compiler_params=PARAMS,
        name="prepare",
    )(in_hbm(listing), in_hbm(traces), in_hbm(own))


def spread(mask_ref, raw_refs, wide, blocks):
    listed, _, members, rows = mask_ref.shape
    start = 0
    for raw_ref in raw_refs:
        flat = raw_ref.shape[0]
        for n in blocks:
            total = jnp.zeros((flat, rows), jnp.bfloat16)
            for m in range(listed):
                mask = (mask_ref[m, n] > 0)[None]
                mask = jnp.broadcast_to(mask, (flat // members, members, rows)).reshape(flat, rows)
                total = jnp.where(mask, raw_ref[:, m * rows : (m + 1) * rows], total)
            wide[start : start + flat, n * rows : (n + 1) * rows] = total
        start += flat


def shifted_sum(p, members, start, taps):
    def tree(first, count):
        if count == 1:
            return p[first * members : (first + 1) * members, :]
        part = count // 2
        return tree(first, part) + roll_left(tree(first + part, part), part)

    return tree(start, taps)


def source_of(route):
    mask, other = route
    return lax.axis_index("tm") ^ jnp.where(lax.axis_index("span") == 0, mask, other)


def correlate(mask_ref, shards, routes, pieces_of_x, wide, ps, lead, local_taps, members, width, add_norm, add_sum):
    _, nblocks, _, rows = mask_ref.shape
    count = len(shards)
    pieces = 4
    blocks, taps = nblocks // pieces, local_taps // pieces

    def widen(n, c):
        spread(mask_ref, shards[n], wide[n % 2], range(c * blocks, (c + 1) * blocks))
        for raw_ref in shards[n]:
            squares = jnp.square(raw_ref[:, c * rows : (c + 1) * rows].astype(jnp.float32))
            add_norm(squares.reshape(-1, members, rows).sum(axis=0))

    def multiply(n, c):
        for start, samples in pieces_of_x[c::pieces]:
            value = samples()
            ps[n % 2][:, lead + start : lead + start + value.shape[1]] = jnp.dot(
                wide[n % 2][...], value, preferred_element_type=jnp.float32
            )

    def shift(n, c, total):
        lines = shifted_sum(ps[n % 2], members, c * taps, taps)
        if c > 0:
            lines = total + roll_left(lines, c * taps)
        if c < pieces - 1:
            return lines
        if lines.shape[1] < width:
            lines = jnp.concatenate([lines, jnp.zeros((members, width - lines.shape[1]), jnp.float32)], axis=1)
        add_sum(pltpu.roll(lines, (width + lead - local_taps * source_of(routes[n])) % width, axis=1))
        return None

    for c in range(pieces):
        widen(0, c)
    for n in range(count + 1):
        total = None
        for c in range(pieces):
            if n + 1 < count:
                widen(n + 1, c)
            if n > 0:
                total = shift(n - 1, c, total)
            if n < count:
                multiply(n, c)


def column_pieces(ref, start):
    size = min(2 * LANES, ref.shape[1])
    return [
        (start + low, lambda low=low: ref[:, low : low + size]) for low in range(0, ref.shape[1], size)
    ]


def absorb(masks, traces, shards, routes, carried, before, local_taps, tap_count):
    shards = [shard if isinstance(shard, list) else [shard] for shard in shards]
    lengths = [len(shard) for shard in shards]
    flat = sum(part.shape[0] for part in shards[0])
    members = flat // local_taps
    channels, lags = traces.shape
    half = tap_count // 2
    width = tap_count + lags

    def kernel(mask_ref, x_ref, *refs):
        inputs = []
        for length in lengths:
            inputs.append(refs[:length])
            refs = refs[length:]
        if carried is not None:
            old_sum, old_norm = refs[:2]
            refs = refs[2:]
        if before is not None:
            before_ref, main_ref, norm_ref, pre_ref, w0, w1, p0, p1, sums = refs
        else:
            sums, norm_ref, w0, w1, p0, p1 = refs
        for p in (p0, p1):
            p[:, :half] = jnp.zeros((flat, half), jnp.float32)
        if carried is None:
            sums[...] = jnp.zeros((members, width), jnp.float32)
            norm_ref[...] = jnp.zeros((members, LANES), jnp.float32)
        else:
            sums[...] = old_sum[...]
            norm_ref[...] = old_norm[...]

        def add_norm(value):
            norm_ref[...] += value

        def add_sum(value):
            sums[...] += value

        correlate(
            mask_ref, inputs, routes, column_pieces(x_ref, 0), (w0, w1), (p0, p1),
            half, local_taps, members, width, add_norm, add_sum,
        )
        if before is not None:
            main_ref[...] = sums[:, tap_count:]
            pre_ref[:members, :] = sums[:, :tap_count]
            pre_ref[members:, :] = before_ref[...]

    scratch = [pltpu.VMEM((flat, channels), jnp.bfloat16)] * 2 + [pltpu.VMEM((flat, half + lags), jnp.float32)] * 2
    norm_shape = pltpu.VMEM((members, LANES), jnp.float32)
    operands = [masks, traces] + [part for shard in shards for part in shard]
    if carried is not None:
        operands += list(carried)
    if before is not None:
        operands.append(before)
        scratch.append(pltpu.VMEM((members, width), jnp.float32))
        shapes = (pltpu.VMEM((members, lags), jnp.float32), norm_shape, pltpu.VMEM((2 * members, tap_count), jnp.float32))
    else:
        shapes = (pltpu.VMEM((members, width), jnp.float32), norm_shape)
    return pl.pallas_call(
        kernel,
        out_shape=shapes,
        in_specs=[VMEM] * len(operands),
        out_specs=(VMEM,) * len(shapes),
        scratch_shapes=scratch,
        compiler_params=PARAMS,
    )(*[resident(value) for value in operands])


def finish(main, norm, energy, after, scale_factor):
    members, lags = main.shape
    tap_count = after.shape[1]
    tail = lags - tap_count

    def kernel(main_ref, norm_ref, energy_ref, after_ref, out_ref):
        norms = jnp.sum(norm_ref[...], axis=1, keepdims=True)
        factor = lax.rsqrt(energy_ref[:, :tail] * norms + epsilon) * scale_factor
        out_ref[:, :tail] = main_ref[:, :tail] * factor
        factor = lax.rsqrt((energy_ref[:, tail:] + after_ref[members:, :]) * norms + epsilon) * scale_factor
        out_ref[:, tail:] = (main_ref[:, tail:] + after_ref[:members, :]) * factor

    return pl.pallas_call(
        kernel,
        out_shape=jax.ShapeDtypeStruct((members, lags), jnp.float32),
        in_specs=[VMEM] * 4,
        compiler_params=PARAMS,
        name="finish",
    )(resident(main), resident(norm), resident(energy), resident(after))


def per_device_chips(traces, templates, blocks):
    channels, _ = traces.shape
    local_taps, members, row_count = templates.shape
    block_rows = row_count // blocks.shape[1]
    nblocks = channels // block_rows
    spans = lax.axis_size("span")
    count = lax.axis_size("tm")
    tap_count = local_taps * count
    both = ("span", "tm")
    listing = blocks.T

    def send(value, target):
        route = []
        for s in range(spans):
            for i in range(count):
                to = target(s, i)
                if to is not None:
                    route.append((s * count + i, to[0] * count + to[1]))
        return lax.ppermute(value, both, route)

    def over_core(value):
        return send(value, lambda s, i: (s, i ^ 1))

    def over_x(value):
        return send(value, lambda s, i: (s, i ^ 2))

    def over_y(value):
        return send(value, lambda s, i: (s ^ 1, i))

    def over_z(value):
        return send(value, lambda s, i: (s, i ^ 4))

    own = templates.reshape(local_taps * members, row_count)
    part = own.shape[0] // 2
    own_route, own_x_route, near_route, near_x_route = (0, 0), (2, 2), (4, 4), (6, 6)
    far_route, far_x_route, far_y_route, far_xy_route = (8, 12), (10, 14), (12, 8), (14, 10)

    def pair(route):
        return [route, (route[0] ^ 1, route[1] ^ 1)]

    state = [None]

    def take(shards, routes, final=None):
        state[0] = absorb(masks, samples, shards, routes, state[0], final, local_taps, tap_count)
        return state[0]

    far = send(own, lambda s, i: (s, i ^ far_route[s]))
    own_x = over_x(own)
    near = over_z(own)
    core_own = over_core(own)
    before, energy, masks, samples, own_here = prepare(listing, traces, own, members, nblocks, tap_count)
    take([own_here, core_own], pair(own_route))
    core_own_x = over_core(own_x)
    near_x = over_z(own_x)
    take([own_x, core_own_x], pair(own_x_route))
    far_x = over_x(far)
    far_y = over_y(far)
    core_near = over_core(near)
    core_far = over_core(far)
    take([near, far], [near_route, far_route])
    take([core_near, core_far], [pair(near_route)[1], pair(far_route)[1]])
    core_near_x = over_core(near_x)
    take([near_x], [near_x_route])
    far_y_part = far_y[:part]
    far_xy_0 = over_x(far_y_part)
    far_x_part = far_x[part:]
    far_xy_1 = over_y(far_x_part)
    core_far_y = over_core(far_y)
    core_far_x = over_core(far_x)
    take([far_x, far_y, core_near_x], [far_x_route, far_y_route, pair(near_x_route)[1]])
    core_far_xy_0 = over_core(far_xy_0)
    core_far_xy_1 = over_core(far_xy_1)
    take([core_far_x, core_far_y], [pair(far_x_route)[1], pair(far_y_route)[1]])
    main, norm, pre = take([[far_xy_0, far_xy_1], [core_far_xy_0, core_far_xy_1]], pair(far_xy_route), before)
    after = send(pre, lambda s, i: (s, i - 1) if i > 0 else None)
    return finish(main, norm, energy, after, math.sqrt(tap_count * row_count))


def fits(mesh, traces, templates, blocks):
    spans, count = mesh.shape["span"], mesh.shape["tm"]
    taps, members, rows = templates.shape
    local_taps = taps // count
    lags = traces.shape[1] // (spans * count)
    block_rows = rows // blocks.shape[1]
    return (
        spans == 2
        and count == 16
        and members == 16
        and local_taps == 16
        and lags % 512 == 0
        and lags >= taps
        and block_rows % 128 == 0
        and traces.shape[0] // block_rows == 8
    )


def solution(mesh):
    def program(traces, templates, blocks):
        chips = fits(mesh, traces, templates, blocks)

        def body(*operands):
            return (per_device_chips if chips else per_device_general)(*operands)

        mapped = jax.shard_map(
            body,
            mesh=mesh,
            in_specs=(P(None, ("span", "tm")), P("tm", None, None), P()),
            out_specs=P(None, ("span", "tm")),
            check_vma=False,
        )
        return mapped(traces, templates, blocks)

    return program
```

```python
import math

import jax
import jax.numpy as jnp
from jax import lax
from jax.experimental import pallas as pl
from jax.experimental.pallas import tpu as pltpu
from jax.sharding import PartitionSpec as P


template_groups = 4
epsilon = 1e-06
LANES = 128


def from_behind(block, axis, distance):
    devices = range(lax.axis_size(axis))
    route = [(i - distance, i) for i in devices if i - distance in devices]
    return lax.ppermute(block, axis, route)


def tap_total(product, lag_count):
    members, tap_count, span_width = product.shape
    flattened = product.reshape(members, tap_count * span_width)
    flattened = jnp.pad(flattened, ((0, 0), (0, tap_count)))
    return flattened.reshape(members, tap_count, span_width + 1)[:, :, :lag_count].sum(axis=1)


def per_device_general(traces, templates, blocks):
    channels, lag_count = traces.shape
    local_taps, members, row_count = templates.shape
    listed = blocks.shape[1]
    block_rows = row_count // listed
    nblocks = channels // block_rows
    tap_count = local_taps * lax.axis_size("tm")
    incoming = from_behind(traces[:, :tap_count], "tm", -1)
    source = jnp.concatenate([traces, incoming], axis=1)
    span_width = source.shape[1]
    squares = (
        jnp.square(source.astype(jnp.float32)).reshape(nblocks, block_rows, span_width).sum(axis=1)
    )
    running = jnp.concatenate(
        [jnp.zeros((nblocks, 1), jnp.float32), jnp.cumsum(squares, axis=1)], axis=1
    )
    window = running[:, tap_count : tap_count + lag_count] - running[:, :lag_count]
    selector = (blocks[:, :, None] == jnp.arange(nblocks, dtype=jnp.int32)[None, None, :]).astype(
        jnp.float32
    )
    counting = selector.sum(axis=1)
    scale_factor = math.sqrt(tap_count * row_count)
    group_size = members // template_groups
    gathered = lax.all_gather(templates, "tm", axis=0, tiled=True)
    pieces = []
    norm_pieces = []
    for group_index in range(template_groups):
        offset = group_index * group_size
        weights = gathered[:, offset : offset + group_size]
        chosen = source.reshape(nblocks, block_rows, span_width)[
            blocks[offset : offset + group_size]
        ]
        chosen = chosen.reshape(group_size, row_count, span_width)
        product = jnp.einsum("kqr,qrl->qkl", weights, chosen, preferred_element_type=jnp.float32)
        pieces.append(tap_total(product, lag_count))
        norm_pieces.append(jnp.sum(jnp.square(weights.astype(jnp.float32)), axis=(0, 2)))
    correlation = jnp.concatenate(pieces, axis=0)
    norm_sums = jnp.concatenate(norm_pieces, axis=0)
    energy = jnp.dot(counting, window, precision=lax.Precision.HIGHEST)
    denominator = energy * norm_sums[:, None] + epsilon
    return correlation * lax.rsqrt(denominator) * scale_factor


SMEM = pl.BlockSpec(memory_space=pltpu.SMEM)
VMEM = pl.BlockSpec(memory_space=pltpu.VMEM)
HBM = pl.BlockSpec(memory_space=pltpu.HBM)
PARAMS = pltpu.CompilerParams(vmem_limit_bytes=24 << 20)


def resident(value):
    return pltpu.with_memory_space_constraint(value, pltpu.VMEM)


def in_hbm(value):
    return pltpu.with_memory_space_constraint(value, pltpu.HBM)


def roll_left(value, distance):
    width = value.shape[-1]
    return pltpu.roll(value, (width - distance) % width, axis=1)


def prepare(listing, traces, own, members, nblocks, tap_count):
    channels, lags = traces.shape
    rows = channels // nblocks
    listed = listing.shape[0]
    width = tap_count + lags

    def kernel(listing_ref, x_hbm, own_hbm, before_ref, energy_ref, mask_ref, x_ref, own_ref, sums, sems):
        copies = [
            pltpu.make_async_copy(x_hbm.at[pl.ds(b * rows, rows)], x_ref.at[pl.ds(b * rows, rows)], sems.at[b])
            for b in range(nblocks)
        ]
        copies.append(pltpu.make_async_copy(own_hbm, own_ref, sems.at[nblocks]))
        for copy in copies:
            copy.start()
        member = lax.broadcasted_iota(jnp.int32, (members, rows), 0)
        for m in range(listed):
            block = jnp.zeros((members, rows), jnp.int32)
            for j in range(members):
                block = jnp.where(member == j, listing_ref[m, j], block)
            for n in range(nblocks):
                mask_ref[m, n] = jnp.where(block == n, 1.0, 0.0).astype(jnp.bfloat16)
        sums[:, :tap_count] = jnp.zeros((nblocks, tap_count), jnp.float32)
        for b in range(nblocks):
            copies[b].wait()
            block = x_ref[b * rows : (b + 1) * rows, :].astype(jnp.float32)
            sums[b : b + 1, tap_count:] = jnp.sum(jnp.square(block), axis=0, keepdims=True)
        total = sums[...]
        distance = 1
        while distance < tap_count:
            total = total + roll_left(total, distance)
            distance *= 2
        sums[...] = total
        for j in range(members):
            energy = sums[pl.ds(listing_ref[0, j], 1), :]
            for m in range(1, listed):
                energy = energy + sums[pl.ds(listing_ref[m, j], 1), :]
            before_ref[j : j + 1, :] = energy[:, :tap_count]
            energy_ref[j : j + 1, :] = energy[:, tap_count:]
        copies[nblocks].wait()

    return pl.pallas_call(
        kernel,
        out_shape=(
            pltpu.VMEM((members, tap_count), jnp.float32),
            pltpu.VMEM((members, lags), jnp.float32),
            pltpu.VMEM((listed, nblocks, members, rows), jnp.bfloat16),
            pltpu.VMEM(traces.shape, traces.dtype),
            pltpu.VMEM(own.shape, own.dtype),
        ),
        in_specs=[SMEM, HBM, HBM],
        out_specs=(VMEM,) * 5,
        scratch_shapes=[pltpu.VMEM((nblocks, width), jnp.float32), pltpu.SemaphoreType.DMA((nblocks + 1,))],
        compiler_params=PARAMS,
        name="prepare",
    )(in_hbm(listing), in_hbm(traces), in_hbm(own))


def spread(mask_ref, raw_refs, wide, blocks):
    listed, _, members, rows = mask_ref.shape
    start = 0
    for raw_ref in raw_refs:
        flat = raw_ref.shape[0]
        for n in blocks:
            tests = [mask_ref[m, n] > 0 for m in range(listed)]
            for t in range(0, flat, members):
                total = jnp.zeros((members, rows), jnp.bfloat16)
                for m in range(listed):
                    total = jnp.where(tests[m], raw_ref[t : t + members, m * rows : (m + 1) * rows], total)
                wide[start + t : start + t + members, n * rows : (n + 1) * rows] = total
        start += flat


def shifted_sum(p, members, start, taps):
    def tree(first, count):
        if count == 1:
            return p[first * members : (first + 1) * members, :]
        part = count // 2
        return tree(first, part) + roll_left(tree(first + part, part), part)

    return tree(start, taps)


def source_of(route):
    mask, other = route
    return lax.axis_index("tm") ^ jnp.where(lax.axis_index("span") == 0, mask, other)


def column_pieces(width):
    size = min(2 * LANES, width)
    return [(low, size) for low in range(0, width, size)]


def absorb(masks, traces, shards, routes, carried, local_taps, tap_count):
    shards = [shard if isinstance(shard, list) else [shard] for shard in shards]
    lengths = [len(shard) for shard in shards]
    flat, rows = sum(part.shape[0] for part in shards[0]), shards[0][0].shape[1]
    members = flat // local_taps
    channels, lags = traces.shape
    half = tap_count // 2
    width = tap_count + lags
    count = len(shards)
    nblocks = masks.shape[1]
    pieces = 4
    blocks, taps = nblocks // pieces, local_taps // pieces
    pending = [] if carried is None else [carried[3]]

    def kernel(mask_ref, x_ref, *refs):
        inputs = []
        for length in lengths:
            inputs.append(refs[:length])
            refs = refs[length:]
        if carried is not None:
            old_sum, old_norm, old_p = refs[:3]
            refs = refs[3:]
        sums, norm_ref, out_p, w0, w1, p0, p1 = refs
        wide, ps = (w0, w1), [(p0, p1)[n % 2] for n in range(count)]
        ps[-1] = out_p
        for p in ps[-2:]:
            p[:, :half] = jnp.zeros((flat, half), jnp.float32)
        if carried is None:
            sums[...] = jnp.zeros((members, width), jnp.float32)
            norm_ref[...] = jnp.zeros((members, LANES), jnp.float32)
        else:
            sums[...] = old_sum[...]
            norm_ref[...] = old_norm[...]
        for p in ps[:-2]:
            p[:, :half] = jnp.zeros((flat, half), jnp.float32)
        waiting = [(old_p, route) for route in pending] + list(zip(ps, routes))

        def widen(n, c):
            spread(mask_ref, inputs[n], wide[n % 2], range(c * blocks, (c + 1) * blocks))

        def measure(n, c):
            for raw_ref in inputs[n]:
                part = raw_ref[:, c * rows // pieces : (c + 1) * rows // pieces]
                squares = jnp.square(part.astype(jnp.float32))
                norm_ref[...] += squares.reshape(-1, members, rows // pieces).sum(axis=0)

        def multiply(n, c):
            for start, size in column_pieces(lags)[c::pieces]:
                ps[n][:, half + start : half + start + size] = jnp.dot(
                    wide[n % 2][...], x_ref[:, start : start + size], preferred_element_type=jnp.float32
                )

        def shift(entry, c, total):
            p, route = entry
            lines = shifted_sum(p, members, c * taps, taps)
            if c > 0:
                lines = total + roll_left(lines, c * taps)
            if c < pieces - 1:
                return lines
            lines = jnp.concatenate([lines, jnp.zeros((members, tap_count - half), jnp.float32)], axis=1)
            distance = (width + half - local_taps * source_of(route)) % width
            sums[...] += pltpu.roll(lines, distance, axis=1)
            return None

        late = len(pending)
        for c in range(pieces):
            widen(0, c)
        for n in range(count):
            entry = n - 1 + late
            total = None
            for c in range(pieces):
                if n + 1 < count:
                    widen(n + 1, c)
                if entry >= 0:
                    total = shift(waiting[entry], c, total)
                multiply(n, c)
                if n == count - 1:
                    for m in range(count):
                        measure(m, c)

    product_shape = pltpu.VMEM((flat, half + lags), jnp.float32)
    scratch = [pltpu.VMEM((flat, channels), jnp.bfloat16)] * 2 + [product_shape] * 2
    norm_shape = pltpu.VMEM((members, LANES), jnp.float32)
    operands = [masks, traces] + [part for shard in shards for part in shard]
    if carried is not None:
        operands += carried[:3]
    shapes = (pltpu.VMEM((members, width), jnp.float32), norm_shape, product_shape)
    results = pl.pallas_call(
        kernel,
        out_shape=shapes,
        in_specs=[VMEM] * len(operands),
        out_specs=(VMEM,) * len(shapes),
        scratch_shapes=scratch,
        compiler_params=PARAMS,
    )(*[resident(value) for value in operands])
    return [*results, routes[-1]]


def place_lines(lines, route, local_taps, tap_count, width):
    members, have = lines.shape
    lines = jnp.concatenate([lines, jnp.zeros((members, width - have), jnp.float32)], axis=1)
    return pltpu.roll(lines, (width + tap_count // 2 - local_taps * source_of(route)) % width, axis=1)


def edge(masks, traces, shards, routes, carried, before, local_taps, tap_count):
    sums, norm, products, route = carried
    flat, rows = sum(part.shape[0] for part in shards[0]), shards[0][0].shape[1]
    members, width = sums.shape
    channels, lags = traces.shape
    half = tap_count // 2
    count = len(shards)
    nblocks = masks.shape[1]
    lengths = [len(shard) for shard in shards]

    def kernel(mask_ref, x_ref, old_sum, old_norm, p_ref, before_ref, *refs):
        inputs = []
        for length in lengths:
            inputs.append(refs[:length])
            refs = refs[length:]
        pre_ref, main_ref, norm_ref = refs[:3]
        wide, ps = refs[3 : 3 + count], refs[3 + count :]
        for p in ps:
            p[:, :half] = jnp.zeros((flat, half), jnp.float32)
        norms = old_norm[...]
        for n in range(count):
            spread(mask_ref, inputs[n], wide[n], range(nblocks))
            ps[n][:, half:] = jnp.dot(wide[n][...], x_ref[:, :tap_count], preferred_element_type=jnp.float32)
            for raw_ref in inputs[n]:
                for low in range(0, rows, LANES):
                    squares = jnp.square(raw_ref[:, low : low + LANES].astype(jnp.float32))
                    norms = norms + squares.reshape(-1, members, LANES).sum(axis=0)
        norm_ref[...] = norms
        lines = place_lines(shifted_sum(p_ref, members, 0, local_taps), route, local_taps, tap_count, width)
        total = old_sum[...] + lines
        main_ref[...] = total[:, tap_count:]
        total = total[:, :tap_count]
        for n in range(count):
            lines = shifted_sum(ps[n], members, 0, local_taps)
            total = total + place_lines(lines, routes[n], local_taps, tap_count, 2 * tap_count)[:, :tap_count]
        pre_ref[:members, :] = total
        pre_ref[members:, :] = before_ref[...]

    operands = [masks, traces, sums, norm, products, before] + [part for shard in shards for part in shard]
    wide_shape = pltpu.VMEM((flat, channels), jnp.bfloat16)
    shapes = (
        pltpu.VMEM((2 * members, tap_count), jnp.float32),
        pltpu.VMEM((members, lags), jnp.float32),
        pltpu.VMEM((members, LANES), jnp.float32),
    ) + (wide_shape,) * count
    return pl.pallas_call(
        kernel,
        out_shape=shapes,
        in_specs=[VMEM] * len(operands),
        out_specs=(VMEM,) * len(shapes),
        scratch_shapes=[pltpu.VMEM((flat, half + tap_count), jnp.float32)] * count,
        compiler_params=PARAMS,
        name="edge",
    )(*[resident(value) for value in operands])


def last(traces, wides, routes, main, local_taps, tap_count):
    flat, _ = wides[0].shape
    members, lags = main.shape
    half = tap_count // 2
    count = len(wides)

    def kernel(x_ref, old_main, *refs):
        wide, main_ref, ps = refs[:count], refs[count], refs[count + 1 :]
        total = old_main[...]
        for n in range(count):
            ps[n][:, :half] = jnp.zeros((flat, half), jnp.float32)
        for n in range(count):
            for start, size in column_pieces(lags):
                ps[n][:, half + start : half + start + size] = jnp.dot(
                    wide[n][...], x_ref[:, start : start + size], preferred_element_type=jnp.float32
                )
        for n in range(count):
            lines = shifted_sum(ps[n], members, 0, local_taps)
            total = total + place_lines(lines, routes[n], local_taps, tap_count, lags + tap_count)[:, tap_count:]
        main_ref[...] = total

    operands = [traces, main, *wides]
    return pl.pallas_call(
        kernel,
        out_shape=pltpu.VMEM((members, lags), jnp.float32),
        in_specs=[VMEM] * len(operands),
        out_specs=VMEM,
        scratch_shapes=[pltpu.VMEM((flat, half + lags), jnp.float32)] * count,
        compiler_params=PARAMS,
        name="last",
    )(*[resident(value) for value in operands])


def finish(main, norm, energy, after, scale_factor):
    members, lags = main.shape
    tap_count = after.shape[1]
    tail = lags - tap_count

    def kernel(main_ref, norm_ref, energy_ref, after_ref, out_ref):
        norms = jnp.sum(norm_ref[...], axis=1, keepdims=True)
        factor = lax.rsqrt(energy_ref[:, :tail] * norms + epsilon) * scale_factor
        out_ref[:, :tail] = main_ref[:, :tail] * factor
        factor = lax.rsqrt((energy_ref[:, tail:] + after_ref[members:, :]) * norms + epsilon) * scale_factor
        out_ref[:, tail:] = (main_ref[:, tail:] + after_ref[:members, :]) * factor

    return pl.pallas_call(
        kernel,
        out_shape=jax.ShapeDtypeStruct((members, lags), jnp.float32),
        in_specs=[VMEM] * 4,
        compiler_params=PARAMS,
        name="finish",
    )(resident(main), resident(norm), resident(energy), resident(after))


def per_device_chips(traces, templates, blocks):
    channels, _ = traces.shape
    local_taps, members, row_count = templates.shape
    block_rows = row_count // blocks.shape[1]
    nblocks = channels // block_rows
    spans = lax.axis_size("span")
    count = lax.axis_size("tm")
    tap_count = local_taps * count
    both = ("span", "tm")
    listing = blocks.T

    def send(value, target):
        route = []
        for s in range(spans):
            for i in range(count):
                to = target(s, i)
                if to is not None:
                    route.append((s * count + i, to[0] * count + to[1]))
        return lax.ppermute(value, both, route)

    def over_core(value):
        return send(value, lambda s, i: (s, i ^ 1))

    def over_x(value):
        return send(value, lambda s, i: (s, i ^ 2))

    def over_y(value):
        return send(value, lambda s, i: (s ^ 1, i))

    def over_z(value):
        return send(value, lambda s, i: (s, i ^ 4))

    own = templates.reshape(local_taps * members, row_count)
    part = own.shape[0] // 2
    own_route, own_x_route, near_route, near_x_route = (0, 0), (2, 2), (4, 4), (6, 6)
    far_route, far_x_route, far_y_route, far_xy_route = (8, 12), (10, 14), (12, 8), (14, 10)

    def pair(route):
        return [route, (route[0] ^ 1, route[1] ^ 1)]

    state = [None]

    def take(shards, routes):
        state[0] = absorb(masks, samples, shards, routes, state[0], local_taps, tap_count)

    far = send(own, lambda s, i: (s, i ^ far_route[s]))
    own_x = over_x(own)
    near = over_z(own)
    core_own = over_core(own)
    before, energy, masks, samples, own_here = prepare(listing, traces, own, members, nblocks, tap_count)
    take([own_here, core_own], pair(own_route))
    core_own_x = over_core(own_x)
    near_x = over_z(own_x)
    take([own_x, core_own_x], pair(own_x_route))
    far_x = over_x(far)
    far_y = over_y(far)
    core_near = over_core(near)
    core_far = over_core(far)
    take([near, far], [near_route, far_route])
    take([core_near, core_far], [pair(near_route)[1], pair(far_route)[1]])
    core_near_x = over_core(near_x)
    take([near_x], [near_x_route])
    far_y_part = far_y[:part]
    far_xy_0 = over_x(far_y_part)
    far_x_part = far_x[part:]
    far_xy_1 = over_y(far_x_part)
    core_far_y = over_core(far_y)
    core_far_x = over_core(far_x)
    take([far_x, far_y, core_near_x], [far_x_route, far_y_route, pair(near_x_route)[1]])
    core_far_xy_0 = over_core(far_xy_0)
    core_far_xy_1 = over_core(far_xy_1)
    take([core_far_x, core_far_y], [pair(far_x_route)[1], pair(far_y_route)[1]])
    ends = [[far_xy_0, far_xy_1], [core_far_xy_0, core_far_xy_1]]
    pre, main, norm, *wides = edge(masks, samples, ends, pair(far_xy_route), state[0], before, local_taps, tap_count)
    after = send(pre, lambda s, i: (s, i - 1) if i > 0 else None)
    main = last(samples, wides, pair(far_xy_route), main, local_taps, tap_count)
    return finish(main, norm, energy, after, math.sqrt(tap_count * row_count))


def fits(mesh, traces, templates, blocks):
    spans, count = mesh.shape["span"], mesh.shape["tm"]
    taps, members, rows = templates.shape
    local_taps = taps // count
    lags = traces.shape[1] // (spans * count)
    block_rows = rows // blocks.shape[1]
    return (
        spans == 2
        and count == 16
        and members == 16
        and local_taps == 16
        and lags % 512 == 0
        and lags >= taps
        and block_rows % 128 == 0
        and traces.shape[0] // block_rows == 8
    )


def solution(mesh):
    def program(traces, templates, blocks):
        chips = fits(mesh, traces, templates, blocks)

        def body(*operands):
            return (per_device_chips if chips else per_device_general)(*operands)

        mapped = jax.shard_map(
            body,
            mesh=mesh,
            in_specs=(P(None, ("span", "tm")), P("tm", None, None), P()),
            out_specs=P(None, ("span", "tm")),
            check_vma=False,
        )
        return mapped(traces, templates, blocks)

    return program
```

```python
import math

import jax
import jax.numpy as jnp
from jax import lax
from jax.experimental import pallas as pl
from jax.experimental.pallas import tpu as pltpu
from jax.sharding import PartitionSpec as P


template_groups = 4
epsilon = 1e-06
LANES = 128


def from_behind(block, axis, distance):
    devices = range(lax.axis_size(axis))
    route = [(i - distance, i) for i in devices if i - distance in devices]
    return lax.ppermute(block, axis, route)


def tap_total(product, lag_count):
    members, tap_count, span_width = product.shape
    flattened = product.reshape(members, tap_count * span_width)
    flattened = jnp.pad(flattened, ((0, 0), (0, tap_count)))
    return flattened.reshape(members, tap_count, span_width + 1)[:, :, :lag_count].sum(axis=1)


def per_device_general(traces, templates, blocks):
    channels, lag_count = traces.shape
    local_taps, members, row_count = templates.shape
    listed = blocks.shape[1]
    block_rows = row_count // listed
    nblocks = channels // block_rows
    tap_count = local_taps * lax.axis_size("tm")
    incoming = from_behind(traces[:, :tap_count], "tm", -1)
    source = jnp.concatenate([traces, incoming], axis=1)
    span_width = source.shape[1]
    squares = (
        jnp.square(source.astype(jnp.float32)).reshape(nblocks, block_rows, span_width).sum(axis=1)
    )
    running = jnp.concatenate(
        [jnp.zeros((nblocks, 1), jnp.float32), jnp.cumsum(squares, axis=1)], axis=1
    )
    window = running[:, tap_count : tap_count + lag_count] - running[:, :lag_count]
    selector = (blocks[:, :, None] == jnp.arange(nblocks, dtype=jnp.int32)[None, None, :]).astype(
        jnp.float32
    )
    counting = selector.sum(axis=1)
    scale_factor = math.sqrt(tap_count * row_count)
    group_size = members // template_groups
    gathered = lax.all_gather(templates, "tm", axis=0, tiled=True)
    pieces = []
    norm_pieces = []
    for group_index in range(template_groups):
        offset = group_index * group_size
        weights = gathered[:, offset : offset + group_size]
        chosen = source.reshape(nblocks, block_rows, span_width)[
            blocks[offset : offset + group_size]
        ]
        chosen = chosen.reshape(group_size, row_count, span_width)
        product = jnp.einsum("kqr,qrl->qkl", weights, chosen, preferred_element_type=jnp.float32)
        pieces.append(tap_total(product, lag_count))
        norm_pieces.append(jnp.sum(jnp.square(weights.astype(jnp.float32)), axis=(0, 2)))
    correlation = jnp.concatenate(pieces, axis=0)
    norm_sums = jnp.concatenate(norm_pieces, axis=0)
    energy = jnp.dot(counting, window, precision=lax.Precision.HIGHEST)
    denominator = energy * norm_sums[:, None] + epsilon
    return correlation * lax.rsqrt(denominator) * scale_factor


SMEM = pl.BlockSpec(memory_space=pltpu.SMEM)
VMEM = pl.BlockSpec(memory_space=pltpu.VMEM)
HBM = pl.BlockSpec(memory_space=pltpu.HBM)
PARAMS = pltpu.CompilerParams(vmem_limit_bytes=24 << 20)


def resident(value):
    return pltpu.with_memory_space_constraint(value, pltpu.VMEM)


def in_hbm(value):
    return pltpu.with_memory_space_constraint(value, pltpu.HBM)


def roll_left(value, distance):
    width = value.shape[-1]
    return pltpu.roll(value, (width - distance) % width, axis=1)


def prepare(listing, traces, own, members, nblocks, tap_count):
    channels, lags = traces.shape
    rows = channels // nblocks
    listed = listing.shape[0]
    width = tap_count + lags

    def kernel(listing_ref, x_hbm, own_hbm, before_ref, energy_ref, mask_ref, x_ref, own_ref, sums, sems):
        copies = [
            pltpu.make_async_copy(x_hbm.at[pl.ds(b * rows, rows)], x_ref.at[pl.ds(b * rows, rows)], sems.at[b])
            for b in range(nblocks)
        ]
        copies.append(pltpu.make_async_copy(own_hbm, own_ref, sems.at[nblocks]))
        for copy in copies:
            copy.start()
        member = lax.broadcasted_iota(jnp.int32, (members, rows), 0)
        for m in range(listed):
            block = jnp.zeros((members, rows), jnp.int32)
            for j in range(members):
                block = jnp.where(member == j, listing_ref[m, j], block)
            for n in range(nblocks):
                mask_ref[m, n] = jnp.where(block == n, 1.0, 0.0).astype(jnp.bfloat16)
        sums[:, :tap_count] = jnp.zeros((nblocks, tap_count), jnp.float32)
        for b in range(nblocks):
            copies[b].wait()
            block = x_ref[b * rows : (b + 1) * rows, :].astype(jnp.float32)
            sums[b : b + 1, tap_count:] = jnp.sum(jnp.square(block), axis=0, keepdims=True)
        total = sums[...]
        distance = 1
        while distance < tap_count:
            total = total + roll_left(total, distance)
            distance *= 2
        sums[...] = total
        for j in range(members):
            energy = sums[pl.ds(listing_ref[0, j], 1), :]
            for m in range(1, listed):
                energy = energy + sums[pl.ds(listing_ref[m, j], 1), :]
            before_ref[j : j + 1, :] = energy[:, :tap_count]
            energy_ref[j : j + 1, :] = energy[:, tap_count:]
        copies[nblocks].wait()

    return pl.pallas_call(
        kernel,
        out_shape=(
            pltpu.VMEM((members, tap_count), jnp.float32),
            pltpu.VMEM((members, lags), jnp.float32),
            pltpu.VMEM((listed, nblocks, members, rows), jnp.bfloat16),
            pltpu.VMEM(traces.shape, traces.dtype),
            pltpu.VMEM(own.shape, own.dtype),
        ),
        in_specs=[SMEM, HBM, HBM],
        out_specs=(VMEM,) * 5,
        scratch_shapes=[pltpu.VMEM((nblocks, width), jnp.float32), pltpu.SemaphoreType.DMA((nblocks + 1,))],
        compiler_params=PARAMS,
        name="prepare",
    )(in_hbm(listing), in_hbm(traces), in_hbm(own))


def spread(mask_ref, raw_refs, wide, blocks):
    listed, _, members, rows = mask_ref.shape
    start = 0
    for raw_ref in raw_refs:
        flat = raw_ref.shape[0]
        for n in blocks:
            tests = [mask_ref[m, n] > 0 for m in range(listed)]
            for t in range(0, flat, members):
                total = jnp.zeros((members, rows), jnp.bfloat16)
                for m in range(listed):
                    total = jnp.where(tests[m], raw_ref[t : t + members, m * rows : (m + 1) * rows], total)
                wide[start + t : start + t + members, n * rows : (n + 1) * rows] = total
        start += flat


def shifted_sum(p, members, start, taps):
    def tree(first, count):
        if count == 1:
            return p[first * members : (first + 1) * members, :]
        part = count // 2
        return tree(first, part) + roll_left(tree(first + part, part), part)

    return tree(start, taps)


def source_of(route):
    mask, other = route
    return lax.axis_index("tm") ^ jnp.where(lax.axis_index("span") == 0, mask, other)


def column_pieces(width):
    size = min(2 * LANES, width)
    return [(low, size) for low in range(0, width, size)]


def absorb(masks, traces, shards, routes, carried, local_taps, tap_count):
    shards = [shard if isinstance(shard, list) else [shard] for shard in shards]
    lengths = [len(shard) for shard in shards]
    flat, rows = sum(part.shape[0] for part in shards[0]), shards[0][0].shape[1]
    members = flat // local_taps
    channels, lags = traces.shape
    half = tap_count // 2
    width = tap_count + lags
    count = len(shards)
    nblocks = masks.shape[1]
    pieces = 4
    blocks, taps = nblocks // pieces, local_taps // pieces
    pending = [] if carried is None else [carried[3]]

    def kernel(mask_ref, x_ref, *refs):
        inputs = []
        for length in lengths:
            inputs.append(refs[:length])
            refs = refs[length:]
        if carried is not None:
            old_sum, old_norm, old_p = refs[:3]
            refs = refs[3:]
        sums, norm_ref, out_p, w0, w1, p0, p1 = refs
        wide, ps = (w0, w1), [(p0, p1)[n % 2] for n in range(count)]
        ps[-1] = out_p
        for p in ps[-2:]:
            p[:, :half] = jnp.zeros((flat, half), jnp.float32)
        if carried is None:
            sums[...] = jnp.zeros((members, width), jnp.float32)
            norm_ref[...] = jnp.zeros((members, LANES), jnp.float32)
        else:
            sums[...] = old_sum[...]
            norm_ref[...] = old_norm[...]
        for p in ps[:-2]:
            p[:, :half] = jnp.zeros((flat, half), jnp.float32)
        waiting = [(old_p, route) for route in pending] + list(zip(ps, routes))

        def widen(n, c):
            spread(mask_ref, inputs[n], wide[n % 2], range(c * blocks, (c + 1) * blocks))

        def measure(n, c):
            for raw_ref in inputs[n]:
                part = raw_ref[:, c * rows // pieces : (c + 1) * rows // pieces]
                squares = jnp.square(part.astype(jnp.float32))
                norm_ref[...] += squares.reshape(-1, members, rows // pieces).sum(axis=0)

        def multiply(n, c):
            for start, size in column_pieces(lags)[c::pieces]:
                ps[n][:, half + start : half + start + size] = jnp.dot(
                    wide[n % 2][...], x_ref[:, start : start + size], preferred_element_type=jnp.float32
                )

        def shift(entry, c, total):
            p, route = entry
            lines = shifted_sum(p, members, c * taps, taps)
            if c > 0:
                lines = total + roll_left(lines, c * taps)
            if c < pieces - 1:
                return lines
            lines = jnp.concatenate([lines, jnp.zeros((members, tap_count - half), jnp.float32)], axis=1)
            distance = (width + half - local_taps * source_of(route)) % width
            sums[...] += pltpu.roll(lines, distance, axis=1)
            return None

        late = len(pending)
        for c in range(pieces):
            widen(0, c)
        for n in range(count):
            entry = n - 1 + late
            total = None
            for c in range(pieces):
                if n + 1 < count:
                    widen(n + 1, c)
                if entry >= 0:
                    total = shift(waiting[entry], c, total)
                multiply(n, c)
                if n == count - 1:
                    for m in range(count):
                        measure(m, c)

    product_shape = pltpu.VMEM((flat, half + lags), jnp.float32)
    scratch = [pltpu.VMEM((flat, channels), jnp.bfloat16)] * 2 + [product_shape] * 2
    norm_shape = pltpu.VMEM((members, LANES), jnp.float32)
    operands = [masks, traces] + [part for shard in shards for part in shard]
    if carried is not None:
        operands += carried[:3]
    shapes = (pltpu.VMEM((members, width), jnp.float32), norm_shape, product_shape)
    results = pl.pallas_call(
        kernel,
        out_shape=shapes,
        in_specs=[VMEM] * len(operands),
        out_specs=(VMEM,) * len(shapes),
        scratch_shapes=scratch,
        compiler_params=PARAMS,
    )(*[resident(value) for value in operands])
    return [*results, routes[-1]]


def place_lines(lines, route, local_taps, tap_count, width):
    members, have = lines.shape
    lines = jnp.concatenate([lines, jnp.zeros((members, width - have), jnp.float32)], axis=1)
    return pltpu.roll(lines, (width + tap_count // 2 - local_taps * source_of(route)) % width, axis=1)


def edge(masks, traces, shards, routes, carried, before, local_taps, tap_count):
    sums, _, products, route = carried
    flat = sum(part.shape[0] for part in shards[0])
    members = sums.shape[0]
    channels = traces.shape[0]
    half = tap_count // 2
    count = len(shards)
    nblocks = masks.shape[1]
    lengths = [len(shard) for shard in shards]

    def kernel(mask_ref, x_ref, old_sum, p_ref, before_ref, *refs):
        inputs = []
        for length in lengths:
            inputs.append(refs[:length])
            refs = refs[length:]
        pre_ref, wide, ps = refs[0], refs[1 : 1 + count], refs[1 + count :]
        total = old_sum[:, :tap_count]

        def add(total, p, origin):
            lines = shifted_sum(p.at[:, : half + tap_count], members, 0, local_taps)
            return total + place_lines(lines, origin, local_taps, tap_count, 2 * tap_count)[:, :tap_count]

        for p in ps:
            p[:, :half] = jnp.zeros((flat, half), jnp.float32)
        for n in range(count):
            spread(mask_ref, inputs[n], wide[n], range(nblocks))
            ps[n][:, half:] = jnp.dot(wide[n][...], x_ref[:, :tap_count], preferred_element_type=jnp.float32)
            if n == 0:
                total = add(total, p_ref, route)
        for n in range(count):
            total = add(total, ps[n], routes[n])
        pre_ref[:members, :] = total
        pre_ref[members:, :] = before_ref[...]

    operands = [masks, traces, sums, products, before] + [part for shard in shards for part in shard]
    shapes = (pltpu.VMEM((2 * members, tap_count), jnp.float32),) + (pltpu.VMEM((flat, channels), jnp.bfloat16),) * count
    return pl.pallas_call(
        kernel,
        out_shape=shapes,
        in_specs=[VMEM] * len(operands),
        out_specs=(VMEM,) * len(shapes),
        scratch_shapes=[pltpu.VMEM((flat, half + tap_count), jnp.float32)] * count,
        compiler_params=PARAMS,
        name="edge",
    )(*[resident(value) for value in operands])


def last(traces, wides, shards, routes, carried, local_taps, tap_count):
    sums, norm, products, route = carried
    flat, _ = wides[0].shape
    members, width = sums.shape
    lags = width - tap_count
    half = tap_count // 2
    count = len(wides)
    parts = [part for shard in shards for part in shard]
    rows = parts[0].shape[1]

    def kernel(x_ref, old_sum, old_norm, p_ref, *refs):
        wide, refs = refs[:count], refs[count:]
        inputs, (main_ref, norm_ref, *ps) = refs[: len(parts)], refs[len(parts) :]
        for n in range(count):
            ps[n][:, :half] = jnp.zeros((flat, half), jnp.float32)

        def add(p, origin):
            lines = shifted_sum(p, members, 0, local_taps)
            main_ref[...] += place_lines(lines, origin, local_taps, tap_count, width)[:, tap_count:]

        main_ref[...] = old_sum[:, tap_count:]
        norms = old_norm[...]
        for n in range(count):
            for start, size in column_pieces(lags):
                ps[n][:, half + start : half + start + size] = jnp.dot(
                    wide[n][...], x_ref[:, start : start + size], preferred_element_type=jnp.float32
                )
                if n == 0 and start == 0:
                    add(p_ref, route)
            if n == 0:
                for raw_ref in inputs:
                    for low in range(0, rows, LANES):
                        squares = jnp.square(raw_ref[:, low : low + LANES].astype(jnp.float32))
                        norms = norms + squares.reshape(-1, members, LANES).sum(axis=0)
            if n > 0:
                add(ps[n - 1], routes[n - 1])
        norm_ref[...] = norms
        add(ps[count - 1], routes[count - 1])

    operands = [traces, sums, norm, products, *wides, *parts]
    return pl.pallas_call(
        kernel,
        out_shape=(pltpu.VMEM((members, lags), jnp.float32), pltpu.VMEM((members, LANES), jnp.float32)),
        in_specs=[VMEM] * len(operands),
        out_specs=(VMEM, VMEM),
        scratch_shapes=[pltpu.VMEM((flat, half + lags), jnp.float32)] * count,
        compiler_params=PARAMS,
        name="last",
    )(*[resident(value) for value in operands])


def finish(main, norm, energy, after, scale_factor):
    members, lags = main.shape
    tap_count = after.shape[1]
    tail = lags - tap_count

    def kernel(main_ref, norm_ref, energy_ref, after_ref, out_ref):
        norms = jnp.sum(norm_ref[...], axis=1, keepdims=True)
        factor = lax.rsqrt(energy_ref[:, :tail] * norms + epsilon) * scale_factor
        out_ref[:, :tail] = main_ref[:, :tail] * factor
        factor = lax.rsqrt((energy_ref[:, tail:] + after_ref[members:, :]) * norms + epsilon) * scale_factor
        out_ref[:, tail:] = (main_ref[:, tail:] + after_ref[:members, :]) * factor

    return pl.pallas_call(
        kernel,
        out_shape=jax.ShapeDtypeStruct((members, lags), jnp.float32),
        in_specs=[VMEM] * 4,
        compiler_params=PARAMS,
        name="finish",
    )(resident(main), resident(norm), resident(energy), resident(after))


def per_device_chips(traces, templates, blocks):
    channels, _ = traces.shape
    local_taps, members, row_count = templates.shape
    block_rows = row_count // blocks.shape[1]
    nblocks = channels // block_rows
    spans = lax.axis_size("span")
    count = lax.axis_size("tm")
    tap_count = local_taps * count
    both = ("span", "tm")
    listing = blocks.T

    def send(value, target):
        route = []
        for s in range(spans):
            for i in range(count):
                to = target(s, i)
                if to is not None:
                    route.append((s * count + i, to[0] * count + to[1]))
        return lax.ppermute(value, both, route)

    def over_core(value):
        return send(value, lambda s, i: (s, i ^ 1))

    def over_x(value):
        return send(value, lambda s, i: (s, i ^ 2))

    def over_y(value):
        return send(value, lambda s, i: (s ^ 1, i))

    def over_z(value):
        return send(value, lambda s, i: (s, i ^ 4))

    own = templates.reshape(local_taps * members, row_count)
    part = own.shape[0] * 3 // 8
    own_route, own_x_route, near_route, near_x_route = (0, 0), (2, 2), (4, 4), (6, 6)
    far_route, far_x_route, far_y_route, far_xy_route = (8, 12), (10, 14), (12, 8), (14, 10)

    def pair(route):
        return [route, (route[0] ^ 1, route[1] ^ 1)]

    state = [None]

    def take(shards, routes):
        state[0] = absorb(masks, samples, shards, routes, state[0], local_taps, tap_count)

    far = send(own, lambda s, i: (s, i ^ far_route[s]))
    own_x = over_x(own)
    near = over_z(own)
    core_own = over_core(own)
    before, energy, masks, samples, own_here = prepare(listing, traces, own, members, nblocks, tap_count)
    take([own_here, core_own], pair(own_route))
    core_own_x = over_core(own_x)
    near_x = over_z(own_x)
    take([own_x, core_own_x], pair(own_x_route))
    far_x = over_x(far)
    far_y = over_y(far)
    core_near = over_core(near)
    core_far = over_core(far)
    take([near, far], [near_route, far_route])
    take([core_near, core_far], [pair(near_route)[1], pair(far_route)[1]])
    core_near_x = over_core(near_x)
    take([near_x], [near_x_route])
    far_y_part = far_y[:part]
    far_xy_0 = over_x(far_y_part)
    far_x_part = far_x[part:]
    far_xy_1 = over_y(far_x_part)
    core_far_y = over_core(far_y)
    core_far_x = over_core(far_x)
    take([far_x, far_y, core_near_x], [far_x_route, far_y_route, pair(near_x_route)[1]])
    core_far_xy_0 = over_core(far_xy_0)
    core_far_xy_1 = over_core(far_xy_1)
    take([core_far_x, core_far_y], [pair(far_x_route)[1], pair(far_y_route)[1]])
    ends = [[far_xy_0, far_xy_1], [core_far_xy_0, core_far_xy_1]]
    pre, *wides = edge(
        masks, samples, ends, pair(far_xy_route), state[0], before, local_taps, tap_count
    )
    after = send(pre, lambda s, i: (s, i - 1) if i > 0 else None)
    main, norm = last(samples, wides, ends, pair(far_xy_route), state[0], local_taps, tap_count)
    return finish(main, norm, energy, after, math.sqrt(tap_count * row_count))


def fits(mesh, traces, templates, blocks):
    spans, count = mesh.shape["span"], mesh.shape["tm"]
    taps, members, rows = templates.shape
    local_taps = taps // count
    lags = traces.shape[1] // (spans * count)
    block_rows = rows // blocks.shape[1]
    return (
        spans == 2
        and count == 16
        and members == 16
        and local_taps == 16
        and lags % 512 == 0
        and lags >= taps
        and block_rows % 128 == 0
        and traces.shape[0] // block_rows == 8
    )


def solution(mesh):
    def program(traces, templates, blocks):
        chips = fits(mesh, traces, templates, blocks)

        def body(*operands):
            return (per_device_chips if chips else per_device_general)(*operands)

        mapped = jax.shard_map(
            body,
            mesh=mesh,
            in_specs=(P(None, ("span", "tm")), P("tm", None, None), P()),
            out_specs=P(None, ("span", "tm")),
            check_vma=False,
        )
        return mapped(traces, templates, blocks)

    return program
```

```python
import math

import jax
import jax.numpy as jnp
from jax import lax
from jax.experimental import pallas as pl
from jax.experimental.pallas import tpu as pltpu
from jax.sharding import PartitionSpec as P


template_groups = 4
epsilon = 1e-06
LANES = 128


def from_behind(block, axis, distance):
    devices = range(lax.axis_size(axis))
    route = [(i - distance, i) for i in devices if i - distance in devices]
    return lax.ppermute(block, axis, route)


def tap_total(product, lag_count):
    members, tap_count, span_width = product.shape
    flattened = product.reshape(members, tap_count * span_width)
    flattened = jnp.pad(flattened, ((0, 0), (0, tap_count)))
    return flattened.reshape(members, tap_count, span_width + 1)[:, :, :lag_count].sum(axis=1)


def per_device_general(traces, templates, blocks):
    channels, lag_count = traces.shape
    local_taps, members, row_count = templates.shape
    listed = blocks.shape[1]
    block_rows = row_count // listed
    nblocks = channels // block_rows
    tap_count = local_taps * lax.axis_size("tm")
    incoming = from_behind(traces[:, :tap_count], "tm", -1)
    source = jnp.concatenate([traces, incoming], axis=1)
    span_width = source.shape[1]
    squares = (
        jnp.square(source.astype(jnp.float32)).reshape(nblocks, block_rows, span_width).sum(axis=1)
    )
    running = jnp.concatenate(
        [jnp.zeros((nblocks, 1), jnp.float32), jnp.cumsum(squares, axis=1)], axis=1
    )
    window = running[:, tap_count : tap_count + lag_count] - running[:, :lag_count]
    selector = (blocks[:, :, None] == jnp.arange(nblocks, dtype=jnp.int32)[None, None, :]).astype(
        jnp.float32
    )
    counting = selector.sum(axis=1)
    scale_factor = math.sqrt(tap_count * row_count)
    group_size = members // template_groups
    gathered = lax.all_gather(templates, "tm", axis=0, tiled=True)
    pieces = []
    norm_pieces = []
    for group_index in range(template_groups):
        offset = group_index * group_size
        weights = gathered[:, offset : offset + group_size]
        chosen = source.reshape(nblocks, block_rows, span_width)[
            blocks[offset : offset + group_size]
        ]
        chosen = chosen.reshape(group_size, row_count, span_width)
        product = jnp.einsum("kqr,qrl->qkl", weights, chosen, preferred_element_type=jnp.float32)
        pieces.append(tap_total(product, lag_count))
        norm_pieces.append(jnp.sum(jnp.square(weights.astype(jnp.float32)), axis=(0, 2)))
    correlation = jnp.concatenate(pieces, axis=0)
    norm_sums = jnp.concatenate(norm_pieces, axis=0)
    energy = jnp.dot(counting, window, precision=lax.Precision.HIGHEST)
    denominator = energy * norm_sums[:, None] + epsilon
    return correlation * lax.rsqrt(denominator) * scale_factor


SMEM = pl.BlockSpec(memory_space=pltpu.SMEM)
VMEM = pl.BlockSpec(memory_space=pltpu.VMEM)
HBM = pl.BlockSpec(memory_space=pltpu.HBM)
PARAMS = pltpu.CompilerParams(vmem_limit_bytes=24 << 20)


def resident(value):
    return pltpu.with_memory_space_constraint(value, pltpu.VMEM)


def in_hbm(value):
    return pltpu.with_memory_space_constraint(value, pltpu.HBM)


def roll_left(value, distance):
    width = value.shape[-1]
    return pltpu.roll(value, (width - distance) % width, axis=1)


def prepare(listing, traces, own, members, nblocks, tap_count):
    channels, lags = traces.shape
    rows = channels // nblocks
    listed = listing.shape[0]
    width = tap_count + lags

    def kernel(listing_ref, x_hbm, own_hbm, before_ref, energy_ref, mask_ref, x_ref, own_ref, sums, sems):
        copies = [
            pltpu.make_async_copy(x_hbm.at[pl.ds(b * rows, rows)], x_ref.at[pl.ds(b * rows, rows)], sems.at[b])
            for b in range(nblocks)
        ]
        copies.append(pltpu.make_async_copy(own_hbm, own_ref, sems.at[nblocks]))
        for copy in copies:
            copy.start()
        member = lax.broadcasted_iota(jnp.int32, (members, rows), 0)
        for m in range(listed):
            block = jnp.zeros((members, rows), jnp.int32)
            for j in range(members):
                block = jnp.where(member == j, listing_ref[m, j], block)
            for n in range(nblocks):
                mask_ref[m, n] = jnp.where(block == n, 1.0, 0.0).astype(jnp.bfloat16)
        sums[:, :tap_count] = jnp.zeros((nblocks, tap_count), jnp.float32)
        for b in range(nblocks):
            copies[b].wait()
            block = x_ref[b * rows : (b + 1) * rows, :].astype(jnp.float32)
            sums[b : b + 1, tap_count:] = jnp.sum(jnp.square(block), axis=0, keepdims=True)
        total = sums[...]
        distance = 1
        while distance < tap_count:
            total = total + roll_left(total, distance)
            distance *= 2
        sums[...] = total
        for j in range(members):
            energy = sums[pl.ds(listing_ref[0, j], 1), :]
            for m in range(1, listed):
                energy = energy + sums[pl.ds(listing_ref[m, j], 1), :]
            before_ref[j : j + 1, :] = energy[:, :tap_count]
            energy_ref[j : j + 1, :] = energy[:, tap_count:]
        copies[nblocks].wait()

    return pl.pallas_call(
        kernel,
        out_shape=(
            pltpu.VMEM((members, tap_count), jnp.float32),
            pltpu.VMEM((members, lags), jnp.float32),
            pltpu.VMEM((listed, nblocks, members, rows), jnp.bfloat16),
            pltpu.VMEM(traces.shape, traces.dtype),
            pltpu.VMEM(own.shape, own.dtype),
        ),
        in_specs=[SMEM, HBM, HBM],
        out_specs=(VMEM,) * 5,
        scratch_shapes=[pltpu.VMEM((nblocks, width), jnp.float32), pltpu.SemaphoreType.DMA((nblocks + 1,))],
        compiler_params=PARAMS,
        name="prepare",
    )(in_hbm(listing), in_hbm(traces), in_hbm(own))


def spread(mask_ref, raw_refs, wide, blocks):
    listed, _, members, rows = mask_ref.shape
    start = 0
    for raw_ref in raw_refs:
        flat = raw_ref.shape[0]
        for n in blocks:
            tests = [mask_ref[m, n] > 0 for m in range(listed)]
            for t in range(0, flat, members):
                total = jnp.zeros((members, rows), jnp.bfloat16)
                for m in range(listed):
                    total = jnp.where(tests[m], raw_ref[t : t + members, m * rows : (m + 1) * rows], total)
                wide[start + t : start + t + members, n * rows : (n + 1) * rows] = total
        start += flat


def shifted_sum(p, members, start, taps):
    def tree(first, count):
        if count == 1:
            return p[first * members : (first + 1) * members, :]
        part = count // 2
        return tree(first, part) + roll_left(tree(first + part, part), part)

    return tree(start, taps)


def source_of(route):
    mask, other = route
    return lax.axis_index("tm") ^ jnp.where(lax.axis_index("span") == 0, mask, other)


def column_pieces(width):
    size = min(2 * LANES, width)
    return [(low, size) for low in range(0, width, size)]


def absorb(masks, traces, shards, routes, carried, local_taps, tap_count):
    shards = [shard if isinstance(shard, list) else [shard] for shard in shards]
    lengths = [len(shard) for shard in shards]
    flat, rows = sum(part.shape[0] for part in shards[0]), shards[0][0].shape[1]
    members = flat // local_taps
    channels, lags = traces.shape
    half = tap_count // 2
    width = tap_count + lags
    count = len(shards)
    nblocks = masks.shape[1]
    pieces = 4
    blocks, taps = nblocks // pieces, local_taps // pieces
    pending = [] if carried is None else [carried[3]]

    def kernel(mask_ref, x_ref, *refs):
        inputs = []
        for length in lengths:
            inputs.append(refs[:length])
            refs = refs[length:]
        if carried is not None:
            old_sum, old_norm, old_p = refs[:3]
            refs = refs[3:]
        sums, norm_ref, out_p, w0, w1, p0, p1 = refs
        wide, ps = (w0, w1), [(p0, p1)[n % 2] for n in range(count)]
        ps[-1] = out_p
        for p in ps[-2:]:
            p[:, :half] = jnp.zeros((flat, half), jnp.float32)
        if carried is None:
            sums[...] = jnp.zeros((members, width), jnp.float32)
            norm_ref[...] = jnp.zeros((members, LANES), jnp.float32)
        else:
            sums[...] = old_sum[...]
            norm_ref[...] = old_norm[...]
        for p in ps[:-2]:
            p[:, :half] = jnp.zeros((flat, half), jnp.float32)
        waiting = [(old_p, route) for route in pending] + list(zip(ps, routes))

        def widen(n, c):
            spread(mask_ref, inputs[n], wide[n % 2], range(c * blocks, (c + 1) * blocks))

        def measure(n, c):
            for raw_ref in inputs[n]:
                part = raw_ref[:, c * rows // pieces : (c + 1) * rows // pieces]
                squares = jnp.square(part.astype(jnp.float32))
                norm_ref[...] += squares.reshape(-1, members, rows // pieces).sum(axis=0)

        def multiply(n, c):
            for start, size in column_pieces(lags)[c::pieces]:
                ps[n][:, half + start : half + start + size] = jnp.dot(
                    wide[n % 2][...], x_ref[:, start : start + size], preferred_element_type=jnp.float32
                )

        def shift(entry, c, total):
            p, route = entry
            lines = shifted_sum(p, members, c * taps, taps)
            if c > 0:
                lines = total + roll_left(lines, c * taps)
            if c < pieces - 1:
                return lines
            lines = jnp.concatenate([lines, jnp.zeros((members, tap_count - half), jnp.float32)], axis=1)
            distance = (width + half - local_taps * source_of(route)) % width
            sums[...] += pltpu.roll(lines, distance, axis=1)
            return None

        late = len(pending)
        for c in range(pieces):
            widen(0, c)
        for n in range(count):
            entry = n - 1 + late
            total = None
            for c in range(pieces):
                if n + 1 < count:
                    widen(n + 1, c)
                if entry >= 0:
                    total = shift(waiting[entry], c, total)
                multiply(n, c)
                if n == count - 1:
                    for m in range(count):
                        measure(m, c)

    product_shape = pltpu.VMEM((flat, half + lags), jnp.float32)
    scratch = [pltpu.VMEM((flat, channels), jnp.bfloat16)] * 2 + [product_shape] * 2
    norm_shape = pltpu.VMEM((members, LANES), jnp.float32)
    operands = [masks, traces] + [part for shard in shards for part in shard]
    if carried is not None:
        operands += carried[:3]
    shapes = (pltpu.VMEM((members, width), jnp.float32), norm_shape, product_shape)
    results = pl.pallas_call(
        kernel,
        out_shape=shapes,
        in_specs=[VMEM] * len(operands),
        out_specs=(VMEM,) * len(shapes),
        scratch_shapes=scratch,
        compiler_params=PARAMS,
    )(*[resident(value) for value in operands])
    return [*results, routes[-1]]


def place_lines(lines, route, local_taps, tap_count, width):
    members, have = lines.shape
    lines = jnp.concatenate([lines, jnp.zeros((members, width - have), jnp.float32)], axis=1)
    return pltpu.roll(lines, (width + tap_count // 2 - local_taps * source_of(route)) % width, axis=1)


def edge(masks, traces, shards, routes, carried, before, local_taps, tap_count):
    sums, _, products, route = carried
    flat = sum(part.shape[0] for part in shards[0])
    members = sums.shape[0]
    channels = traces.shape[0]
    half = tap_count // 2
    count = len(shards)
    nblocks = masks.shape[1]
    lengths = [len(shard) for shard in shards]

    def kernel(mask_ref, x_ref, old_sum, p_ref, before_ref, *refs):
        inputs = []
        for length in lengths:
            inputs.append(refs[:length])
            refs = refs[length:]
        pre_ref, wide, ps = refs[0], refs[1 : 1 + count], refs[1 + count :]
        total = old_sum[:, :tap_count]

        def add(total, p, origin):
            lines = shifted_sum(p.at[:, : half + tap_count], members, 0, local_taps)
            return total + place_lines(lines, origin, local_taps, tap_count, 2 * tap_count)[:, :tap_count]

        for p in ps:
            p[:, :half] = jnp.zeros((flat, half), jnp.float32)
        for n in range(count):
            spread(mask_ref, inputs[n], wide[n], range(nblocks))
            ps[n][:, half:] = jnp.dot(wide[n][...], x_ref[:, :tap_count], preferred_element_type=jnp.float32)
            if n == 0:
                total = add(total, p_ref, route)
        for n in range(count):
            total = add(total, ps[n], routes[n])
        pre_ref[:members, :] = total
        pre_ref[members:, :] = before_ref[...]

    operands = [masks, traces, sums, products, before] + [part for shard in shards for part in shard]
    shapes = (pltpu.VMEM((2 * members, tap_count), jnp.float32),) + (pltpu.VMEM((flat, channels), jnp.bfloat16),) * count
    return pl.pallas_call(
        kernel,
        out_shape=shapes,
        in_specs=[VMEM] * len(operands),
        out_specs=(VMEM,) * len(shapes),
        scratch_shapes=[pltpu.VMEM((flat, half + tap_count), jnp.float32)] * count,
        compiler_params=PARAMS,
        name="edge",
    )(*[resident(value) for value in operands])


def last(traces, wides, shards, routes, carried, local_taps, tap_count):
    sums, norm, products, route = carried
    flat, _ = wides[0].shape
    members, width = sums.shape
    lags = width - tap_count
    half = tap_count // 2
    count = len(wides)
    parts = [part for shard in shards for part in shard]
    rows = parts[0].shape[1]

    def kernel(x_ref, old_sum, old_norm, p_ref, *refs):
        wide, refs = refs[:count], refs[count:]
        inputs, (main_ref, norm_ref, *ps) = refs[: len(parts)], refs[len(parts) :]
        for n in range(count):
            ps[n][:, :half] = jnp.zeros((flat, half), jnp.float32)

        def add(p, origin):
            lines = shifted_sum(p, members, 0, local_taps)
            main_ref[...] += place_lines(lines, origin, local_taps, tap_count, width)[:, tap_count:]

        main_ref[...] = old_sum[:, tap_count:]
        norms = old_norm[...]
        for n in range(count):
            for start, size in column_pieces(lags):
                ps[n][:, half + start : half + start + size] = jnp.dot(
                    wide[n][...], x_ref[:, start : start + size], preferred_element_type=jnp.float32
                )
                if n == 0 and start == 0:
                    add(p_ref, route)
            if n == 0:
                for raw_ref in inputs:
                    for low in range(0, rows, LANES):
                        squares = jnp.square(raw_ref[:, low : low + LANES].astype(jnp.float32))
                        norms = norms + squares.reshape(-1, members, LANES).sum(axis=0)
            if n > 0:
                add(ps[n - 1], routes[n - 1])
        norm_ref[...] = norms
        add(ps[count - 1], routes[count - 1])

    operands = [traces, sums, norm, products, *wides, *parts]
    return pl.pallas_call(
        kernel,
        out_shape=(pltpu.VMEM((members, lags), jnp.float32), pltpu.VMEM((members, LANES), jnp.float32)),
        in_specs=[VMEM] * len(operands),
        out_specs=(VMEM, VMEM),
        scratch_shapes=[pltpu.VMEM((flat, half + lags), jnp.float32)] * count,
        compiler_params=PARAMS,
        name="last",
    )(*[resident(value) for value in operands])


def finish(main, norm, energy, after_core, after_chip, scale_factor):
    members, lags = main.shape
    tap_count = after_core.shape[1]
    tail = lags - tap_count

    def kernel(main_ref, norm_ref, energy_ref, core_ref, chip_ref, out_ref):
        after = jnp.where(lax.axis_index("tm") % 2 == 0, core_ref[...], chip_ref[...])
        norms = jnp.sum(norm_ref[...], axis=1, keepdims=True)
        factor = lax.rsqrt(energy_ref[:, :tail] * norms + epsilon) * scale_factor
        out_ref[:, :tail] = main_ref[:, :tail] * factor
        factor = lax.rsqrt((energy_ref[:, tail:] + after[members:, :]) * norms + epsilon) * scale_factor
        out_ref[:, tail:] = (main_ref[:, tail:] + after[:members, :]) * factor

    return pl.pallas_call(
        kernel,
        out_shape=jax.ShapeDtypeStruct((members, lags), jnp.float32),
        in_specs=[VMEM] * 5,
        compiler_params=PARAMS,
        name="finish",
    )(resident(main), resident(norm), resident(energy), resident(after_core), resident(after_chip))


def per_device_chips(traces, templates, blocks):
    channels, _ = traces.shape
    local_taps, members, row_count = templates.shape
    block_rows = row_count // blocks.shape[1]
    nblocks = channels // block_rows
    spans = lax.axis_size("span")
    count = lax.axis_size("tm")
    tap_count = local_taps * count
    both = ("span", "tm")
    listing = blocks.T

    def send(value, target):
        route = []
        for s in range(spans):
            for i in range(count):
                to = target(s, i)
                if to is not None:
                    route.append((s * count + i, to[0] * count + to[1]))
        return lax.ppermute(value, both, route)

    def over_core(value):
        return send(value, lambda s, i: (s, i ^ 1))

    def over_x(value):
        return send(value, lambda s, i: (s, i ^ 2))

    def over_y(value):
        return send(value, lambda s, i: (s ^ 1, i))

    def over_z(value):
        return send(value, lambda s, i: (s, i ^ 4))

    own = templates.reshape(local_taps * members, row_count)
    part = own.shape[0] * 5 // 8
    own_route, own_x_route, near_route, near_x_route = (0, 0), (2, 2), (4, 4), (6, 6)
    far_route, far_x_route, far_y_route, far_xy_route = (8, 12), (10, 14), (12, 8), (14, 10)

    def pair(route):
        return [route, (route[0] ^ 1, route[1] ^ 1)]

    state = [None]

    def take(shards, routes):
        state[0] = absorb(masks, samples, shards, routes, state[0], local_taps, tap_count)

    far = send(own, lambda s, i: (s, i ^ far_route[s]))
    own_x = over_x(own)
    near = over_z(own)
    core_own = over_core(own)
    before, energy, masks, samples, own_here = prepare(listing, traces, own, members, nblocks, tap_count)
    take([own_here, core_own], pair(own_route))
    core_own_x = over_core(own_x)
    near_x = over_z(own_x)
    take([own_x, core_own_x], pair(own_x_route))
    far_x = over_x(far)
    far_y = over_y(far)
    core_near = over_core(near)
    core_far = over_core(far)
    take([near, far], [near_route, far_route])
    take([core_near, core_far], [pair(near_route)[1], pair(far_route)[1]])
    core_near_x = over_core(near_x)
    take([near_x], [near_x_route])
    far_y_part = far_y[:part]
    far_xy_0 = over_x(far_y_part)
    far_x_part = far_x[part:]
    far_xy_1 = over_y(far_x_part)
    core_far_y = over_core(far_y)
    core_far_x = over_core(far_x)
    take([far_x, far_y, core_near_x], [far_x_route, far_y_route, pair(near_x_route)[1]])
    core_far_xy_0 = over_core(far_xy_0)
    core_far_xy_1 = over_core(far_xy_1)
    take([core_far_x, core_far_y], [pair(far_x_route)[1], pair(far_y_route)[1]])
    ends = [[far_xy_0, far_xy_1], [core_far_xy_0, core_far_xy_1]]
    pre, *wides = edge(
        masks, samples, ends, pair(far_xy_route), state[0], before, local_taps, tap_count
    )
    after_core = over_core(pre)
    after_chip = send(pre, lambda s, i: (s, i - 1) if i > 0 and i % 2 == 0 else None)
    main, norm = last(samples, wides, ends, pair(far_xy_route), state[0], local_taps, tap_count)
    return finish(main, norm, energy, after_core, after_chip, math.sqrt(tap_count * row_count))


def fits(mesh, traces, templates, blocks):
    spans, count = mesh.shape["span"], mesh.shape["tm"]
    taps, members, rows = templates.shape
    local_taps = taps // count
    lags = traces.shape[1] // (spans * count)
    block_rows = rows // blocks.shape[1]
    return (
        spans == 2
        and count == 16
        and members == 16
        and local_taps == 16
        and lags % 512 == 0
        and lags >= taps
        and block_rows % 128 == 0
        and traces.shape[0] // block_rows == 8
    )


def solution(mesh):
    def program(traces, templates, blocks):
        chips = fits(mesh, traces, templates, blocks)

        def body(*operands):
            return (per_device_chips if chips else per_device_general)(*operands)

        mapped = jax.shard_map(
            body,
            mesh=mesh,
            in_specs=(P(None, ("span", "tm")), P("tm", None, None), P()),
            out_specs=P(None, ("span", "tm")),
            check_vma=False,
        )
        return mapped(traces, templates, blocks)

    return program
```
